32 devices in a mesh: tm: 8 (over y, x, core), space: 4 (over z).
Axes of the slice: x: 2, y: 2, z: 4, core: 2. Of those that a mesh axis runs over, the one named last changes fastest.
Arguments:
- states_old: float32 [8, 41, 32768], P('tm', None, 'space'), may hold values from -6 to 6
- coupling: float32 [256, 2, 128, 128], P('space'), may hold values from 0 to 0.1
- gate_center: float32 [40, 1], replicated, may hold values from -1 to 1
- gate_slope: float32 [40, 1], replicated, may hold values from 0.3 to 1
- gate_rate: float32 [40, 1], replicated, may hold values from 0.02 to 2
- reversal: float32 [40, 1], replicated, may hold values from -2 to 2
- conductance: float32 [40, 32768], P(None, 'space'), may hold values from 0.001 to 0.03
- stimulus: float32 [8, 32768], P('tm', 'space'), may hold values from -3 to 3
- coarse_rate: float32 [41, 32768], P(None, 'space'), may hold values from 0.025 to 1.25
Outputs:
- states_new: float32 [8, 41, 32768], P('tm', None, 'space')
- voltage_new: float32 [8, 32768], P('tm', 'space')
The draws below stay inside these ranges and needn't reach their ends.
All inputs are finite; a program needn't handle non-finite values.
Results may differ from the reference program's by a relative error of at most 0.0003.
Values sent between devices are 32-bit elements; how exact they have to be, the bound alone decides.
No kernel may reach another device: no remote copies, remote signals or barrier semaphores. Data moves between devices by JAX's collectives and lax.ppermute only.
A program may use at most 192 MiB of HBM per device.

```python
import math
import jax
import jax.numpy as jnp
from jax import lax

STATES = 41
GATES = 40
TILE = 128
FINE = 2
SUB = 2
CG_ITERS = 8
NBLK = 256
NODES = 32768
SLICES = 8


def shard_levels(key, shape, pieces, least, high):
    gain = 1.0
    for position, shards_of in pieces:
        heights = jax.random.uniform(jax.random.fold_in(jax.random.fold_in(key, 6), position), (shards_of,), jnp.float32, least / len(pieces), high / len(pieces))
        gain = gain * jnp.repeat(jnp.exp(heights), shape[position] // shards_of).reshape((-1,) + (1,) * (len(shape) - 1 - position))
    return gain


def gaussian(own_key, extent, scale, limit, pieces=(), held_as=jnp.bfloat16):
    entries = scale * jax.random.normal(own_key, extent, jnp.float32)
    if pieces:
        entries = entries * shard_levels(own_key, extent, pieces, -0.22, 0.18)
    return jnp.clip(entries, -limit, limit).astype(held_as)


def setup_inputs(seed: int = 0) -> dict:
    seeds = jax.random.split(jax.random.key(seed), 10)
    return {
        "states_old": gaussian(seeds[0], (SLICES, STATES, NODES), 1.0, 6.0, ((0, 8), (2, 4)), jnp.float32),
        "coupling": jnp.clip(0.1 * jax.random.uniform(seeds[1], (NBLK, 2, TILE, TILE), jnp.float32) ** shard_levels(seeds[1], (NBLK, 2, TILE, TILE), ((0, 4),), -0.2, 0.2), 0.0, 0.1),
        "gate_center": jnp.clip(jax.random.uniform(seeds[2], (GATES, 1), jnp.float32, -1.0, 1.0), -1.0, 1.0),
        "gate_slope": jnp.clip(jax.random.uniform(seeds[3], (GATES, 1), jnp.float32, 0.3, 1.0), 0.3, 1.0),
        "gate_rate": jnp.clip(jnp.exp(jax.random.uniform(seeds[4], (GATES, 1), jnp.float32, math.log(0.02), math.log(2.0))), 0.02, 2.0),
        "reversal": jnp.clip(jax.random.uniform(seeds[5], (GATES, 1), jnp.float32, -2.0, 2.0), -2.0, 2.0),
        "conductance": jnp.clip(jnp.exp(math.log(0.03) - 3.4011973 * jax.random.uniform(seeds[6], (GATES, NODES), jnp.float32) ** shard_levels(seeds[6], (GATES, NODES), ((1, 4),), -0.2, 0.2)), 0.001, 0.03),
        "stimulus": gaussian(seeds[7], (SLICES, NODES), 0.5, 3.0, ((0, 8), (1, 4)), jnp.float32),
        "coarse_rate": jnp.clip(jnp.exp(math.log(1.25) - 3.912023 * jax.random.uniform(seeds[8], (STATES, NODES), jnp.float32) ** shard_levels(seeds[8], (STATES, NODES), ((1, 4),), -0.2, 0.2)), 0.025, 1.25),
    }


HIGHEST_PRECISION = lax.Precision.HIGHEST


def ionic_update(voltage, gating, conductance, gate_center, gate_slope, gate_rate, reversal):
    for substep in range(SUB):
        steady = jax.nn.sigmoid((voltage[None, :] - gate_center) / gate_slope)
        damping = jnp.exp(-gate_rate * (0.5 + steady))
        gating = steady + (gating - steady) * damping
        current = jnp.sum(conductance * gating * (voltage[None, :] - reversal), axis=0)
        voltage = voltage - current
    return voltage, gating


def couple_all(vector, coupling):
    blocks = vector.shape[0]
    tile_width = vector.shape[1]
    extended = jnp.concatenate([vector, jnp.zeros((2, tile_width), jnp.float32)], axis=0)
    ahead_sum = jnp.einsum("bik,bk->bi", coupling[:, 0], extended[1:blocks + 1], precision=HIGHEST_PRECISION) + jnp.einsum("bik,bk->bi", coupling[:, 1], extended[2:blocks + 2], precision=HIGHEST_PRECISION)
    carried = jnp.einsum("bjki,bk->bji", coupling, vector, precision=HIGHEST_PRECISION)
    behind = jnp.concatenate([jnp.zeros((1, tile_width), jnp.float32), carried[:-1, 0]], axis=0) + jnp.concatenate([jnp.zeros((2, tile_width), jnp.float32), carried[:-2, 1]], axis=0)
    return ahead_sum + behind


def solve_all(right_side, degree, coupling):
    def operate(vector):
        return vector + degree * vector - couple_all(vector, coupling)

    iterate = right_side
    residual = right_side - operate(right_side)
    direction = residual
    norm_now = jnp.sum(residual * residual)
    for iteration in range(CG_ITERS):
        mapped = operate(direction)
        step_size = norm_now / jnp.sum(direction * mapped)
        iterate = iterate + step_size * direction
        residual = residual - step_size * mapped
        norm_next = jnp.sum(residual * residual)
        direction = residual + (norm_next / norm_now) * direction
        norm_now = norm_next
    return iterate


def reference(states_old, coupling, gate_center, gate_slope, gate_rate, reversal, conductance, stimulus, coarse_rate):
    degree = couple_all(jnp.ones((NBLK, TILE), jnp.float32), coupling)

    def fine_slice(slice_pair):
        state, pacing = slice_pair
        voltage = state[0]
        gating = state[1:]
        for fine_step in range(FINE):
            voltage, gating = ionic_update(voltage, gating, conductance, gate_center, gate_slope, gate_rate, reversal)
            voltage = voltage + pacing
            voltage = solve_all(voltage.reshape(NBLK, TILE), degree, coupling).reshape(-1)
        return jnp.concatenate([voltage[None, :], gating], axis=0)

    fine_state = lax.map(fine_slice, (states_old, stimulus))
    factor = jnp.exp(-coarse_rate[None, :, :] * (1.0 + jax.nn.sigmoid(states_old[:, 0]))[:, None, :])
    offset = fine_state - factor * states_old
    loop_a = jnp.ones_like(factor[0])
    loop_r = jnp.zeros_like(offset[0])
    for slice_index in range(SLICES):
        loop_a = factor[slice_index] * loop_a
        loop_r = factor[slice_index] * loop_r + offset[slice_index]
    current = loop_r / (1.0 - loop_a)
    results = []
    for slice_index in range(SLICES):
        results.append(current)
        current = factor[slice_index] * current + offset[slice_index]
    states_new = jnp.stack(results)
    return states_new, states_new[:, 0]
```

```python
import jax
import jax.numpy as jnp
from jax import lax
from jax.sharding import PartitionSpec as P

FINE = 2
SUB = 2
CG_ITERS = 8


def passed_along(value, axis, steps):
    count = lax.axis_size(axis)
    leading, last = (max(0, -steps), min(count, count - steps))
    return lax.ppermute(value, axis, [(source, source + steps) for source in range(leading, last)])


def shifted(value, axis, steps):
    count = lax.axis_size(axis)
    return lax.ppermute(value, axis, [(source, (source + steps) % count) for source in range(count)])


def exchange(partials, axis, down=None, up=None):
    count = lax.axis_size(axis)
    mine = lax.axis_index(axis)
    width = partials.shape[0]
    row = jnp.zeros((1, 128), jnp.float32).at[0, :width].set(partials)
    received = [row]
    got_down = None
    got_up = None
    for steps in range(1, count):
        pieces = [row]
        if steps == 1 and down is not None:
            pieces.append(down)
        if steps == count - 1 and up is not None:
            pieces.append(up)
        payload = jnp.concatenate(pieces, axis=0) if len(pieces) > 1 else row
        arrived = shifted(payload, axis, steps)
        received.append(arrived[:1])
        offset = 1
        if steps == 1 and down is not None:
            got_down = arrived[offset : offset + down.shape[0]]
            offset += down.shape[0]
        if steps == count - 1 and up is not None:
            got_up = arrived[offset : offset + up.shape[0]]
    stacked = jnp.concatenate(received, axis=0)[:, :width]
    order = (mine - jnp.arange(count)) % count
    by_source = jnp.take(stacked, order, axis=0)
    total = by_source[0]
    for source in range(1, count):
        total = total + by_source[source]
    if got_down is not None:
        got_down = jnp.where(mine == 0, jnp.zeros_like(got_down), got_down)
    if got_up is not None:
        got_up = jnp.where(mine == count - 1, jnp.zeros_like(got_up), got_up)
    return total, got_down, got_up


def ionic_update(voltage, gating, conductance, gate_center, gate_slope, gate_rate, reversal):
    for substep in range(SUB):
        steady = jax.nn.sigmoid((voltage[None, :] - gate_center) / gate_slope)
        damping = jnp.exp(-gate_rate * (0.5 + steady))
        gating = steady + (gating - steady) * damping
        current = jnp.sum(conductance * gating * (voltage[None, :] - reversal), axis=0)
        voltage = voltage - current
    return (voltage, gating)


def body(
    states_old,
    coupling,
    gate_center,
    gate_slope,
    gate_rate,
    reversal,
    conductance,
    stimulus,
    coarse_rate,
):
    num_blocks = coupling.shape[0]
    tile_width = coupling.shape[2]
    zero_rows = jnp.zeros((2, tile_width), jnp.float32)

    def couple_local(vector, upper_rows):
        extended = jnp.concatenate([vector, upper_rows], axis=0)
        ahead_sum = jnp.sum(
            coupling[:, 0] * extended[1 : num_blocks + 1, None, :]
            + coupling[:, 1] * extended[2 : num_blocks + 2, None, :],
            axis=-1,
        )
        carried = jnp.sum(coupling * vector[:, None, :, None], axis=2)
        inner = jnp.concatenate([zero_rows[:1], carried[:-1, 0]], axis=0) + jnp.concatenate(
            [zero_rows, carried[:-2, 1]], axis=0
        )
        spilled = jnp.stack([carried[-1, 0] + carried[-2, 1], carried[-1, 1]])
        return ahead_sum + inner, spilled

    def pad_head(rows):
        return jnp.concatenate(
            [rows, jnp.zeros((num_blocks - 2, tile_width), jnp.float32)], axis=0
        )

    ones = jnp.ones((num_blocks, tile_width), jnp.float32)
    local_degree, spilled = couple_local(ones, passed_along(ones[:2], "space", -1))
    degree = local_degree + pad_head(passed_along(spilled, "space", 1))

    voltage = states_old[0, 0]
    gating = states_old[0, 1:]
    for fine_step in range(FINE):
        voltage, gating = ionic_update(
            voltage, gating, conductance, gate_center, gate_slope, gate_rate, reversal
        )
        voltage = voltage + stimulus[0]
        right_side = voltage.reshape(num_blocks, tile_width)
        iterate = right_side
        upper = passed_along(right_side[:2], "space", -1)
        partial, spilled = couple_local(right_side, upper)
        arrived = passed_along(spilled, "space", 1)
        mapped = right_side + degree * right_side - partial - pad_head(arrived)
        residual = right_side - mapped
        norm_now, _, residual_up = exchange(
            jnp.sum(residual * residual)[None], "space", up=residual[:2]
        )
        norm_now = norm_now[0]
        direction = residual
        direction_up = residual_up
        for iteration in range(CG_ITERS):
            partial, spilled = couple_local(direction, direction_up)
            local_mapped = direction + degree * direction - partial
            curvature_part = jnp.sum(direction * local_mapped) - jnp.sum(direction_up * spilled)
            curvature, arrived, _ = exchange(curvature_part[None], "space", down=spilled)
            mapped = local_mapped - pad_head(arrived)
            step_size = norm_now / curvature[0]
            iterate = iterate + step_size * direction
            residual = residual - step_size * mapped
            norm_next, _, residual_up = exchange(
                jnp.sum(residual * residual)[None], "space", up=residual[:2]
            )
            norm_next = norm_next[0]
            direction = residual + norm_next / norm_now * direction
            direction_up = residual_up + norm_next / norm_now * direction_up
            norm_now = norm_next
        voltage = iterate.reshape(-1)
    fine_state = jnp.concatenate([voltage[None, :], gating], axis=0)
    exponent = 1.0 + jax.nn.sigmoid(states_old[0, 0])
    factor = jnp.exp(-coarse_rate * exponent[None, :])
    offset = fine_state - factor * states_old[0]

    slices = lax.axis_size("tm")
    assert slices & (slices - 1) == 0
    packed = shifted(jnp.concatenate([exponent[None, :], offset], axis=0), "tm", 1)
    span = 1
    while span < slices:
        earlier = shifted(packed, "tm", span)
        decay = jnp.exp(-coarse_rate * packed[0][None, :])
        packed = jnp.concatenate(
            [(packed[0] + earlier[0])[None, :], decay * earlier[1:] + packed[1:]], axis=0
        )
        span *= 2
    loop_a = jnp.exp(-coarse_rate * packed[0][None, :])
    new_state = packed[1:] / (1.0 - loop_a)
    return (new_state[None], new_state[0][None])


def solution(mesh):
    return jax.shard_map(
        body,
        mesh=mesh,
        in_specs=(
            P("tm", None, "space"),
            P("space", None, None, None),
            P(),
            P(),
            P(),
            P(),
            P(None, "space"),
            P("tm", "space"),
            P(None, "space"),
        ),
        out_specs=(P("tm", None, "space"), P("tm", "space")),
        check_vma=False,
    )
```

```python
import jax
import jax.numpy as jnp
from jax import lax
from jax.sharding import PartitionSpec as P

FINE = 2
SUB = 2
CG_ITERS = 8


def passed_along(value, axis, steps):
    count = lax.axis_size(axis)
    leading, last = (max(0, -steps), min(count, count - steps))
    return lax.ppermute(value, axis, [(source, source + steps) for source in range(leading, last)])


def shifted(value, axis, steps):
    count = lax.axis_size(axis)
    return lax.ppermute(value, axis, [(source, (source + steps) % count) for source in range(count)])


def exchange(partials, axis, down, up):
    count = lax.axis_size(axis)
    mine = lax.axis_index(axis)
    width = partials.shape[0]
    row = jnp.zeros((1, 128), jnp.float32).at[0, :width].set(partials)
    received = [row]
    got_down = None
    got_up = None
    for steps in range(1, count):
        pieces = [row]
        if steps == 1:
            pieces.append(down)
        if steps == count - 1:
            pieces.append(up)
        arrived = shifted(jnp.concatenate(pieces, axis=0), axis, steps)
        received.append(arrived[0, :width])
        offset = 1
        if steps == 1:
            got_down = arrived[offset : offset + down.shape[0]]
            offset += down.shape[0]
        if steps == count - 1:
            got_up = arrived[offset : offset + up.shape[0]]
    received[0] = partials
    while len(received) > 1 and len(received) % 2 == 0:
        half = len(received) // 2
        received = [received[k] + received[k + half] for k in range(half)]
    total = received[0]
    for extra in received[1:]:
        total = total + extra
    got_up = jnp.where(mine == count - 1, jnp.zeros_like(got_up), got_up)
    return total, got_down, got_up


def ionic_update(voltage, gating, conductance, gate_center, gate_slope, gate_rate, reversal):
    for substep in range(SUB):
        steady = jax.nn.sigmoid((voltage[None, :] - gate_center) / gate_slope)
        damping = jnp.exp(-gate_rate * (0.5 + steady))
        gating = steady + (gating - steady) * damping
        current = jnp.sum(conductance * gating * (voltage[None, :] - reversal), axis=0)
        voltage = voltage - current
    return (voltage, gating)


def body(
    states_old,
    coupling,
    gate_center,
    gate_slope,
    gate_rate,
    reversal,
    conductance,
    stimulus,
    coarse_rate,
):
    num_blocks = coupling.shape[0]
    tile_width = coupling.shape[2]
    zero_rows = jnp.zeros((2, tile_width), jnp.float32)

    def couple_local(vector, upper_rows):
        extended = jnp.concatenate([vector, upper_rows], axis=0)
        ahead_sum = jnp.sum(
            coupling[:, 0] * extended[1 : num_blocks + 1, None, :]
            + coupling[:, 1] * extended[2 : num_blocks + 2, None, :],
            axis=-1,
        )
        carried = jnp.sum(coupling * vector[:, None, :, None], axis=2)
        inner = jnp.concatenate([zero_rows[:1], carried[:-1, 0]], axis=0) + jnp.concatenate(
            [zero_rows, carried[:-2, 1]], axis=0
        )
        spilled = jnp.stack([carried[-1, 0] + carried[-2, 1], carried[-1, 1]])
        return ahead_sum + inner, spilled

    def pad_head(rows):
        return jnp.concatenate(
            [rows, jnp.zeros((num_blocks - 2, tile_width), jnp.float32)], axis=0
        )

    space_count = lax.axis_size("space")
    on_last = lax.axis_index("space") == space_count - 1

    def couple_part(vector, upper_rows):
        partial, spilled = couple_local(vector, upper_rows)
        return partial, jnp.where(on_last, jnp.zeros_like(spilled), spilled)

    ones = jnp.ones((num_blocks, tile_width), jnp.float32)
    local_degree, spilled = couple_part(ones, passed_along(ones[:2], "space", -1))
    degree = local_degree + pad_head(passed_along(spilled, "space", 1))

    def solve(right_side, side_steps=()):
        side_steps = list(side_steps)
        side_state = None
        upper = passed_along(right_side[:2], "space", -1)
        partial, spilled = couple_part(right_side, upper)
        local_mapped = right_side + degree * right_side - partial
        arrived = passed_along(spilled, "space", 1)
        mapped_up = passed_along(local_mapped[:2], "space", -1) - spilled
        residual = right_side - (local_mapped - pad_head(arrived))
        residual_up = upper - mapped_up
        iterate = right_side
        for iteration in range(CG_ITERS):
            partial, spilled = couple_part(residual, residual_up)
            local_image = residual + degree * residual - partial
            norm_part = jnp.sum(residual * residual)
            energy_part = jnp.sum(residual * local_image) - jnp.sum(residual_up * spilled)
            sums, arrived, image_up = exchange(
                jnp.stack([norm_part, energy_part]), "space", spilled, local_image[:2]
            )
            norm_now, energy = sums[0], sums[1]
            image = local_image - pad_head(arrived)
            image_up = image_up - spilled
            if iteration == 0:
                step_size = norm_now / energy
                direction, direction_up = residual, residual_up
                mapped, mapped_up = image, image_up
            else:
                ratio = norm_now / norm_before
                step_size = norm_now / (energy - ratio * norm_now / step_before)
                direction = residual + ratio * direction
                direction_up = residual_up + ratio * direction_up
                mapped = image + ratio * mapped
                mapped_up = image_up + ratio * mapped_up
            iterate = iterate + step_size * direction
            residual = residual - step_size * mapped
            residual_up = residual_up - step_size * mapped_up
            norm_before, step_before = norm_now, step_size
            if side_steps and iteration % 2 == 0:
                side_state = side_steps.pop(0)(side_state)
            if side_state is not None and iteration % 2 == 1:
                side_state, residual, residual_up, iterate = lax.optimization_barrier(
                    (side_state, residual, residual_up, iterate)
                )
        for step in side_steps:
            side_state = step(side_state)
        return iterate, side_state

    slices = lax.axis_size("tm")
    assert slices & (slices - 1) == 0

    def scan_steps(rows, rates, exponent):
        def first(_):
            return shifted(jnp.concatenate([exponent[None, :], rows], axis=0), "tm", 1)

        def doubling(span):
            def step(packed):
                earlier = shifted(packed, "tm", span)
                decay = jnp.exp(-rates * packed[0][None, :])
                return jnp.concatenate(
                    [(packed[0] + earlier[0])[None, :], decay * earlier[1:] + packed[1:]],
                    axis=0,
                )

            return step

        steps = [first]
        span = 1
        while span < slices:
            steps.append(doubling(span))
            span *= 2
        return steps

    def cyclic_scan(rows, rates, exponent):
        packed = None
        for step in scan_steps(rows, rates, exponent):
            packed = step(packed)
        return packed[1:], packed[0]

    exponent = 1.0 + jax.nn.sigmoid(states_old[0, 0])
    factor = jnp.exp(-coarse_rate * exponent[None, :])

    voltage = states_old[0, 0]
    gating = states_old[0, 1:]
    for fine_step in range(FINE):
        voltage, gating = ionic_update(
            voltage, gating, conductance, gate_center, gate_slope, gate_rate, reversal
        )
        side_steps = ()
        if fine_step == FINE - 1:
            side_steps = scan_steps(
                gating - factor[1:] * states_old[0, 1:], coarse_rate[1:], exponent
            )
        voltage = voltage + stimulus[0]
        voltage, gating_scan = solve(voltage.reshape(num_blocks, tile_width), side_steps)
        voltage = voltage.reshape(-1)
    gating_rows = gating_scan[1:]
    voltage_offset = voltage - factor[0] * states_old[0, 0]
    voltage_row, total_exponent = cyclic_scan(voltage_offset[None, :], coarse_rate[:1], exponent)
    loop_a = jnp.exp(-coarse_rate * total_exponent[None, :])
    new_state = jnp.concatenate([voltage_row, gating_rows], axis=0) / (1.0 - loop_a)
    return (new_state[None], new_state[0][None])


def solution(mesh):
    return jax.shard_map(
        body,
        mesh=mesh,
        in_specs=(
            P("tm", None, "space"),
            P("space", None, None, None),
            P(),
            P(),
            P(),
            P(),
            P(None, "space"),
            P("tm", "space"),
            P(None, "space"),
        ),
        out_specs=(P("tm", None, "space"), P("tm", "space")),
        check_vma=False,
    )
```

```python
import jax
import jax.numpy as jnp
from jax import lax
from jax.experimental import pallas as pl
from jax.experimental.pallas import tpu as pltpu
from jax.sharding import PartitionSpec as P

FINE = 2
SUB = 2
CG_ITERS = 8
GROUP = 8


def couple_kernel(v_ref, vt_ref, c_ref, ahead_ref, carried_ref):
    g = pl.program_id(0)
    for t in range(GROUP):
        b = g * GROUP + t
        c0 = c_ref[t, 0]
        c1 = c_ref[t, 1]
        prod = c0 * v_ref[pl.ds(b + 1, 1), :] + c1 * v_ref[pl.ds(b + 2, 1), :]
        ahead_ref[0, :, t : t + 1] = jnp.sum(prod, axis=1, keepdims=True)
        col = vt_ref[0, :, t : t + 1]
        carried_ref[t, 0:1, :] = jnp.sum(c0 * col, axis=0, keepdims=True)
        carried_ref[t, 1:2, :] = jnp.sum(c1 * col, axis=0, keepdims=True)


def couple_call(extended, coupling):
    blocks, width = coupling.shape[0], coupling.shape[2]
    groups = blocks // GROUP
    columns = extended[:blocks].reshape(groups, GROUP, width).transpose(0, 2, 1)
    ahead_t, carried = pl.pallas_call(
        couple_kernel,
        grid=(groups,),
        in_specs=[
            pl.BlockSpec((blocks + 2, width), lambda g: (0, 0)),
            pl.BlockSpec((1, width, GROUP), lambda g: (g, 0, 0)),
            pl.BlockSpec((GROUP, 2, width, width), lambda g: (g, 0, 0, 0)),
        ],
        out_specs=[
            pl.BlockSpec((1, width, GROUP), lambda g: (g, 0, 0)),
            pl.BlockSpec((GROUP, 2, width), lambda g: (g, 0, 0)),
        ],
        out_shape=[
            jax.ShapeDtypeStruct((groups, width, GROUP), jnp.float32),
            jax.ShapeDtypeStruct((blocks, 2, width), jnp.float32),
        ],
        cost_estimate=pl.CostEstimate(
            flops=8 * blocks * width * width,
            transcendentals=0,
            bytes_accessed=4 * blocks * 2 * width * width,
        ),
    )(extended, columns, coupling)
    return ahead_t.transpose(0, 2, 1).reshape(blocks, width), carried


def passed_along(value, axis, steps):
    count = lax.axis_size(axis)
    leading, last = (max(0, -steps), min(count, count - steps))
    return lax.ppermute(value, axis, [(source, source + steps) for source in range(leading, last)])


def shifted(value, axis, steps):
    count = lax.axis_size(axis)
    return lax.ppermute(value, axis, [(source, (source + steps) % count) for source in range(count)])


def exchange(partials, axis, down, up):
    count = lax.axis_size(axis)
    mine = lax.axis_index(axis)
    width = partials.shape[0]
    row = jnp.zeros((1, 128), jnp.float32).at[0, :width].set(partials)
    received = [row]
    got_down = None
    got_up = None
    for steps in range(1, count):
        pieces = [row]
        if steps == 1:
            pieces.append(down)
        if steps == count - 1:
            pieces.append(up)
        arrived = shifted(jnp.concatenate(pieces, axis=0), axis, steps)
        received.append(arrived[0, :width])
        offset = 1
        if steps == 1:
            got_down = arrived[offset : offset + down.shape[0]]
            offset += down.shape[0]
        if steps == count - 1:
            got_up = arrived[offset : offset + up.shape[0]]
    received[0] = partials
    while len(received) > 1 and len(received) % 2 == 0:
        half = len(received) // 2
        received = [received[k] + received[k + half] for k in range(half)]
    total = received[0]
    for extra in received[1:]:
        total = total + extra
    got_up = jnp.where(mine == count - 1, jnp.zeros_like(got_up), got_up)
    return total, got_down, got_up


def ionic_update(voltage, gating, conductance, gate_center, gate_slope, gate_rate, reversal):
    for substep in range(SUB):
        steady = jax.nn.sigmoid((voltage[None, :] - gate_center) / gate_slope)
        damping = jnp.exp(-gate_rate * (0.5 + steady))
        gating = steady + (gating - steady) * damping
        current = jnp.sum(conductance * gating * (voltage[None, :] - reversal), axis=0)
        voltage = voltage - current
    return (voltage, gating)


def body(
    states_old,
    coupling,
    gate_center,
    gate_slope,
    gate_rate,
    reversal,
    conductance,
    stimulus,
    coarse_rate,
):
    num_blocks = coupling.shape[0]
    tile_width = coupling.shape[2]
    zero_rows = jnp.zeros((2, tile_width), jnp.float32)

    def couple_local(vector, upper_rows):
        extended = jnp.concatenate([vector, upper_rows], axis=0)
        ahead_sum, carried = couple_call(extended, coupling)
        inner = jnp.concatenate([zero_rows[:1], carried[:-1, 0]], axis=0) + jnp.concatenate(
            [zero_rows, carried[:-2, 1]], axis=0
        )
        spilled = jnp.stack([carried[-1, 0] + carried[-2, 1], carried[-1, 1]])
        return ahead_sum + inner, spilled

    def pad_head(rows):
        return jnp.concatenate(
            [rows, jnp.zeros((num_blocks - 2, tile_width), jnp.float32)], axis=0
        )

    space_count = lax.axis_size("space")
    on_last = lax.axis_index("space") == space_count - 1

    def couple_part(vector, upper_rows):
        partial, spilled = couple_local(vector, upper_rows)
        return partial, jnp.where(on_last, jnp.zeros_like(spilled), spilled)

    ones = jnp.ones((num_blocks, tile_width), jnp.float32)
    local_degree, spilled = couple_part(ones, passed_along(ones[:2], "space", -1))
    degree = local_degree + pad_head(passed_along(spilled, "space", 1))

    def solve(right_side, side_steps=()):
        side_steps = list(side_steps)
        side_state = None
        upper = passed_along(right_side[:2], "space", -1)
        partial, spilled = couple_part(right_side, upper)
        local_mapped = right_side + degree * right_side - partial
        arrived = passed_along(spilled, "space", 1)
        mapped_up = passed_along(local_mapped[:2], "space", -1) - spilled
        residual = right_side - (local_mapped - pad_head(arrived))
        residual_up = upper - mapped_up
        iterate = right_side
        for iteration in range(CG_ITERS):
            partial, spilled = couple_part(residual, residual_up)
            local_image = residual + degree * residual - partial
            norm_part = jnp.sum(residual * residual)
            energy_part = jnp.sum(residual * local_image) - jnp.sum(residual_up * spilled)
            sums, arrived, image_up = exchange(
                jnp.stack([norm_part, energy_part]), "space", spilled, local_image[:2]
            )
            norm_now, energy = sums[0], sums[1]
            image = local_image - pad_head(arrived)
            image_up = image_up - spilled
            if iteration == 0:
                step_size = norm_now / energy
                direction, direction_up = residual, residual_up
                mapped, mapped_up = image, image_up
            else:
                ratio = norm_now / norm_before
                step_size = norm_now / (energy - ratio * norm_now / step_before)
                direction = residual + ratio * direction
                direction_up = residual_up + ratio * direction_up
                mapped = image + ratio * mapped
                mapped_up = image_up + ratio * mapped_up
            iterate = iterate + step_size * direction
            residual = residual - step_size * mapped
            residual_up = residual_up - step_size * mapped_up
            norm_before, step_before = norm_now, step_size
            if side_steps and iteration % 2 == 0:
                side_state = side_steps.pop(0)(side_state)
            if side_state is not None and iteration % 2 == 1:
                side_state, residual, residual_up, iterate = lax.optimization_barrier(
                    (side_state, residual, residual_up, iterate)
                )
        for step in side_steps:
            side_state = step(side_state)
        return iterate, side_state

    slices = lax.axis_size("tm")
    assert slices & (slices - 1) == 0

    def scan_steps(rows, rates, exponent):
        def first(_):
            return shifted(jnp.concatenate([exponent[None, :], rows], axis=0), "tm", 1)

        def doubling(span):
            def step(packed):
                earlier = shifted(packed, "tm", span)
                decay = jnp.exp(-rates * packed[0][None, :])
                return jnp.concatenate(
                    [(packed[0] + earlier[0])[None, :], decay * earlier[1:] + packed[1:]],
                    axis=0,
                )

            return step

        steps = [first]
        span = 1
        while span < slices:
            steps.append(doubling(span))
            span *= 2
        return steps

    def cyclic_scan(rows, rates, exponent):
        packed = None
        for step in scan_steps(rows, rates, exponent):
            packed = step(packed)
        return packed[1:], packed[0]

    exponent = 1.0 + jax.nn.sigmoid(states_old[0, 0])
    factor = jnp.exp(-coarse_rate * exponent[None, :])

    voltage = states_old[0, 0]
    gating = states_old[0, 1:]
    for fine_step in range(FINE):
        voltage, gating = ionic_update(
            voltage, gating, conductance, gate_center, gate_slope, gate_rate, reversal
        )
        side_steps = ()
        if fine_step == FINE - 1:
            side_steps = scan_steps(
                gating - factor[1:] * states_old[0, 1:], coarse_rate[1:], exponent
            )
        voltage = voltage + stimulus[0]
        voltage, gating_scan = solve(voltage.reshape(num_blocks, tile_width), side_steps)
        voltage = voltage.reshape(-1)
    gating_rows = gating_scan[1:]
    voltage_offset = voltage - factor[0] * states_old[0, 0]
    voltage_row, total_exponent = cyclic_scan(voltage_offset[None, :], coarse_rate[:1], exponent)
    loop_a = jnp.exp(-coarse_rate * total_exponent[None, :])
    new_state = jnp.concatenate([voltage_row, gating_rows], axis=0) / (1.0 - loop_a)
    return (new_state[None], new_state[0][None])


def solution(mesh):
    return jax.shard_map(
        body,
        mesh=mesh,
        in_specs=(
            P("tm", None, "space"),
            P("space", None, None, None),
            P(),
            P(),
            P(),
            P(),
            P(None, "space"),
            P("tm", "space"),
            P(None, "space"),
        ),
        out_specs=(P("tm", None, "space"), P("tm", "space")),
        check_vma=False,
    )
```

```python
import jax
import jax.numpy as jnp
from jax import lax
from jax.sharding import PartitionSpec as P

FINE = 2
SUB = 2
CG_ITERS = 8


def passed_along(value, axis, steps):
    count = lax.axis_size(axis)
    leading, last = (max(0, -steps), min(count, count - steps))
    return lax.ppermute(value, axis, [(source, source + steps) for source in range(leading, last)])


def shifted(value, axis, steps):
    count = lax.axis_size(axis)
    return lax.ppermute(value, axis, [(source, (source + steps) % count) for source in range(count)])


def sum_over(partials, axis):
    count = lax.axis_size(axis)
    received = [partials]
    for steps in range(1, count):
        received.append(shifted(partials[None, :], axis, steps)[0])
    while len(received) > 1 and len(received) % 2 == 0:
        half = len(received) // 2
        received = [received[k] + received[k + half] for k in range(half)]
    total = received[0]
    for extra in received[1:]:
        total = total + extra
    return total


def ionic_update(voltage, gating, conductance, gate_center, gate_slope, gate_rate, reversal):
    for substep in range(SUB):
        steady = jax.nn.sigmoid((voltage[None, :] - gate_center) / gate_slope)
        damping = jnp.exp(-gate_rate * (0.5 + steady))
        gating = steady + (gating - steady) * damping
        current = jnp.sum(conductance * gating * (voltage[None, :] - reversal), axis=0)
        voltage = voltage - current
    return (voltage, gating)


def body(
    states_old,
    coupling,
    gate_center,
    gate_slope,
    gate_rate,
    reversal,
    conductance,
    stimulus,
    coarse_rate,
):
    num_blocks = coupling.shape[0]
    tile_width = coupling.shape[2]
    zero_rows = jnp.zeros((2, tile_width), jnp.float32)

    def couple_local(vector, upper_rows):
        extended = jnp.concatenate([vector, upper_rows], axis=0)
        ahead_sum = jnp.sum(
            coupling[:, 0] * extended[1 : num_blocks + 1, None, :]
            + coupling[:, 1] * extended[2 : num_blocks + 2, None, :],
            axis=-1,
        )
        carried = jnp.sum(coupling * vector[:, None, :, None], axis=2)
        inner = jnp.concatenate([zero_rows[:1], carried[:-1, 0]], axis=0) + jnp.concatenate(
            [zero_rows, carried[:-2, 1]], axis=0
        )
        spilled = jnp.stack([carried[-1, 0] + carried[-2, 1], carried[-1, 1]])
        return ahead_sum + inner, spilled

    def pad_head(rows):
        return jnp.concatenate(
            [rows, jnp.zeros((num_blocks - 2, tile_width), jnp.float32)], axis=0
        )

    space_count = lax.axis_size("space")
    on_last = lax.axis_index("space") == space_count - 1

    def couple_part(vector, upper_rows):
        partial, spilled = couple_local(vector, upper_rows)
        return partial, jnp.where(on_last, jnp.zeros_like(spilled), spilled)

    ones = jnp.ones((num_blocks, tile_width), jnp.float32)
    local_degree, spilled = couple_part(ones, passed_along(ones[:2], "space", -1))
    degree = local_degree + pad_head(passed_along(spilled, "space", 1))

    def apply(vector, vector_up):
        partial, spilled = couple_part(vector, vector_up)
        local_image = vector + degree * vector - partial
        head = vector[:2] + degree[:2] * vector[:2] - partial[:2]
        sent_up, sent_down = lax.optimization_barrier((head, spilled))
        image_up = passed_along(sent_up, "space", -1) - spilled
        arrived = passed_along(sent_down, "space", 1)
        return local_image - pad_head(arrived), image_up

    def solve(right_side, side_steps=()):
        side_steps = list(side_steps)
        side_state = None
        upper = passed_along(right_side[:2], "space", -1)
        mapped, mapped_up = apply(right_side, upper)
        residual = right_side - mapped
        residual_up = upper - mapped_up
        image, image_up = apply(residual, residual_up)
        iterate = right_side
        for iteration in range(CG_ITERS):
            sums = sum_over(
                jnp.stack([jnp.sum(residual * residual), jnp.sum(image * residual)]), "space"
            )
            norm_now, energy = sums[0], sums[1]
            second, second_up = apply(image, image_up)
            if iteration == 0:
                step_size = norm_now / energy
                direction = residual
                mapped, mapped_second, mapped_second_up = image, second, second_up
            else:
                ratio = norm_now / norm_before
                step_size = norm_now / (energy - ratio * norm_now / step_before)
                direction = residual + ratio * direction
                mapped = image + ratio * mapped
                mapped_second = second + ratio * mapped_second
                mapped_second_up = second_up + ratio * mapped_second_up
            iterate = iterate + step_size * direction
            residual = residual - step_size * mapped
            image = image - step_size * mapped_second
            image_up = image_up - step_size * mapped_second_up
            norm_before, step_before = norm_now, step_size
            if side_steps and iteration % 2 == 0:
                side_state = side_steps.pop(0)(side_state)
            if side_state is not None and iteration % 2 == 1:
                side_state, residual, image, image_up, iterate = lax.optimization_barrier(
                    (side_state, residual, image, image_up, iterate)
                )
        for step in side_steps:
            side_state = step(side_state)
        return iterate, side_state

    slices = lax.axis_size("tm")
    assert slices & (slices - 1) == 0

    def scan_steps(rows, rates, exponent):
        def first(_):
            return shifted(jnp.concatenate([exponent[None, :], rows], axis=0), "tm", 1)

        def doubling(span):
            def step(packed):
                earlier = shifted(packed, "tm", span)
                decay = jnp.exp(-rates * packed[0][None, :])
                return jnp.concatenate(
                    [(packed[0] + earlier[0])[None, :], decay * earlier[1:] + packed[1:]],
                    axis=0,
                )

            return step

        steps = [first]
        span = 1
        while span < slices:
            steps.append(doubling(span))
            span *= 2
        return steps

    def cyclic_scan(rows, rates, exponent):
        packed = None
        for step in scan_steps(rows, rates, exponent):
            packed = step(packed)
        return packed[1:], packed[0]

    exponent = 1.0 + jax.nn.sigmoid(states_old[0, 0])
    factor = jnp.exp(-coarse_rate * exponent[None, :])

    voltage = states_old[0, 0]
    gating = states_old[0, 1:]
    for fine_step in range(FINE):
        voltage, gating = ionic_update(
            voltage, gating, conductance, gate_center, gate_slope, gate_rate, reversal
        )
        side_steps = ()
        if fine_step == FINE - 1:
            side_steps = scan_steps(
                gating - factor[1:] * states_old[0, 1:], coarse_rate[1:], exponent
            )
        voltage = voltage + stimulus[0]
        voltage, gating_scan = solve(voltage.reshape(num_blocks, tile_width), side_steps)
        voltage = voltage.reshape(-1)
    gating_rows = gating_scan[1:]
    voltage_offset = voltage - factor[0] * states_old[0, 0]
    voltage_row, total_exponent = cyclic_scan(voltage_offset[None, :], coarse_rate[:1], exponent)
    loop_a = jnp.exp(-coarse_rate * total_exponent[None, :])
    new_state = jnp.concatenate([voltage_row, gating_rows], axis=0) / (1.0 - loop_a)
    return (new_state[None], new_state[0][None])


def solution(mesh):
    return jax.shard_map(
        body,
        mesh=mesh,
        in_specs=(
            P("tm", None, "space"),
            P("space", None, None, None),
            P(),
            P(),
            P(),
            P(),
            P(None, "space"),
            P("tm", "space"),
            P(None, "space"),
        ),
        out_specs=(P("tm", None, "space"), P("tm", "space")),
        check_vma=False,
    )
```

```python
import jax
import jax.numpy as jnp
from jax import lax
from jax.sharding import PartitionSpec as P

FINE = 2
SUB = 2
CG_ITERS = 8


def passed_along(value, axis, steps):
    count = lax.axis_size(axis)
    leading, last = (max(0, -steps), min(count, count - steps))
    return lax.ppermute(value, axis, [(source, source + steps) for source in range(leading, last)])


def shifted(value, axis, steps):
    count = lax.axis_size(axis)
    return lax.ppermute(value, axis, [(source, (source + steps) % count) for source in range(count)])


def exchange(partials, axis, down, up):
    count = lax.axis_size(axis)
    width = partials.shape[0]
    received = [partials]
    got_down = None
    got_up = None
    for steps in range(1, count):
        pieces = [partials]
        if steps == 1:
            pieces.append(down)
        if steps == count - 1:
            pieces.append(up)
        arrived = shifted(jnp.concatenate(pieces, axis=0), axis, steps)
        received.append(arrived[:width])
        offset = width
        if steps == 1:
            got_down = arrived[offset : offset + down.shape[0]]
            offset += down.shape[0]
        if steps == count - 1:
            got_up = arrived[offset : offset + up.shape[0]]
    while len(received) > 1 and len(received) % 2 == 0:
        half = len(received) // 2
        received = [received[k] + received[k + half] for k in range(half)]
    total = received[0]
    for extra in received[1:]:
        total = total + extra
    return jnp.sum(total, axis=1), got_down, got_up


def ionic_update(voltage, gating, conductance, gate_center, gate_slope, gate_rate, reversal):
    for substep in range(SUB):
        steady = jax.nn.sigmoid((voltage[None, :] - gate_center) / gate_slope)
        damping = jnp.exp(-gate_rate * (0.5 + steady))
        gating = steady + (gating - steady) * damping
        current = jnp.sum(conductance * gating * (voltage[None, :] - reversal), axis=0)
        voltage = voltage - current
    return (voltage, gating)


def body(
    states_old,
    coupling,
    gate_center,
    gate_slope,
    gate_rate,
    reversal,
    conductance,
    stimulus,
    coarse_rate,
):
    num_blocks = coupling.shape[0]
    tile_width = coupling.shape[2]
    zero_rows = jnp.zeros((2, tile_width), jnp.float32)

    def couple_local(vector, upper_rows):
        extended = jnp.concatenate([vector, upper_rows], axis=0)
        ahead_sum = jnp.sum(
            coupling[:, 0] * extended[1 : num_blocks + 1, None, :]
            + coupling[:, 1] * extended[2 : num_blocks + 2, None, :],
            axis=-1,
        )
        carried = jnp.sum(coupling * vector[:, None, :, None], axis=2)
        inner = jnp.concatenate([zero_rows[:1], carried[:-1, 0]], axis=0) + jnp.concatenate(
            [zero_rows, carried[:-2, 1]], axis=0
        )
        spilled = jnp.stack([carried[-1, 0] + carried[-2, 1], carried[-1, 1]])
        return ahead_sum + inner, spilled

    def pad_head(rows):
        return jnp.concatenate(
            [rows, jnp.zeros((num_blocks - 2, tile_width), jnp.float32)], axis=0
        )

    space_count = lax.axis_size("space")
    on_last = lax.axis_index("space") == space_count - 1
    on_first = lax.axis_index("space") == 0

    def couple_part(vector, upper_rows):
        partial, spilled = couple_local(vector, upper_rows)
        return partial, jnp.where(on_last, jnp.zeros_like(spilled), spilled)

    ones = jnp.ones((num_blocks, tile_width), jnp.float32)
    local_degree, spilled = couple_part(ones, passed_along(ones[:2], "space", -1))
    degree = local_degree + pad_head(passed_along(spilled, "space", 1))

    def solve(right_side, side_steps=()):
        side_steps = list(side_steps)
        side_state = None
        upper = passed_along(right_side[:2], "space", -1)
        partial, spilled = couple_part(right_side, upper)
        local_mapped = right_side + degree * right_side - partial
        arrived = passed_along(spilled, "space", 1)
        mapped_up = passed_along(local_mapped[:2], "space", -1) - spilled
        residual = right_side - (local_mapped - pad_head(arrived))
        residual_up = upper - mapped_up
        iterate = right_side
        for iteration in range(CG_ITERS):
            partial, spilled = couple_part(residual, residual_up)
            local_image = residual + degree * residual - partial
            norm_part = jnp.sum(residual * residual, axis=0)
            energy_part = jnp.sum(residual * local_image, axis=0) - jnp.sum(
                residual_up * spilled, axis=0
            )
            sent_up = jnp.where(on_first, jnp.zeros_like(spilled), local_image[:2])
            sums, arrived, image_up = exchange(
                jnp.stack([norm_part, energy_part]), "space", spilled, sent_up
            )
            norm_now, energy = sums[0], sums[1]
            image = local_image - pad_head(arrived)
            image_up = image_up - spilled
            if iteration == 0:
                step_size = norm_now / energy
                direction, direction_up = residual, residual_up
                mapped, mapped_up = image, image_up
            else:
                ratio = norm_now / norm_before
                step_size = norm_now / (energy - ratio * norm_now / step_before)
                direction = residual + ratio * direction
                direction_up = residual_up + ratio * direction_up
                mapped = image + ratio * mapped
                mapped_up = image_up + ratio * mapped_up
            iterate = iterate + step_size * direction
            residual = residual - step_size * mapped
            residual_up = residual_up - step_size * mapped_up
            norm_before, step_before = norm_now, step_size
            if side_steps and iteration % 2 == 0:
                side_state = side_steps.pop(0)(side_state)
            if side_state is not None and iteration % 2 == 1:
                side_state, residual, residual_up, iterate = lax.optimization_barrier(
                    (side_state, residual, residual_up, iterate)
                )
        for step in side_steps:
            side_state = step(side_state)
        return iterate, side_state

    slices = lax.axis_size("tm")
    assert slices & (slices - 1) == 0

    def scan_steps(rows, rates, exponent):
        def first(_):
            return shifted(jnp.concatenate([exponent[None, :], rows], axis=0), "tm", 1)

        def doubling(span):
            def step(packed):
                earlier = shifted(packed, "tm", span)
                decay = jnp.exp(-rates * packed[0][None, :])
                return jnp.concatenate(
                    [(packed[0] + earlier[0])[None, :], decay * earlier[1:] + packed[1:]],
                    axis=0,
                )

            return step

        steps = [first]
        span = 1
        while span < slices:
            steps.append(doubling(span))
            span *= 2
        return steps

    def cyclic_scan(rows, rates, exponent):
        packed = None
        for step in scan_steps(rows, rates, exponent):
            packed = step(packed)
        return packed[1:], packed[0]

    exponent = 1.0 + jax.nn.sigmoid(states_old[0, 0])
    factor = jnp.exp(-coarse_rate * exponent[None, :])

    voltage = states_old[0, 0]
    gating = states_old[0, 1:]
    for fine_step in range(FINE):
        voltage, gating = ionic_update(
            voltage, gating, conductance, gate_center, gate_slope, gate_rate, reversal
        )
        side_steps = ()
        if fine_step == FINE - 1:
            side_steps = scan_steps(
                gating - factor[1:] * states_old[0, 1:], coarse_rate[1:], exponent
            )
        voltage = voltage + stimulus[0]
        voltage, gating_scan = solve(voltage.reshape(num_blocks, tile_width), side_steps)
        voltage = voltage.reshape(-1)
    gating_rows = gating_scan[1:]
    voltage_offset = voltage - factor[0] * states_old[0, 0]
    voltage_row, total_exponent = cyclic_scan(voltage_offset[None, :], coarse_rate[:1], exponent)
    loop_a = jnp.exp(-coarse_rate * total_exponent[None, :])
    new_state = jnp.concatenate([voltage_row, gating_rows], axis=0) / (1.0 - loop_a)
    return (new_state[None], new_state[0][None])


def solution(mesh):
    return jax.shard_map(
        body,
        mesh=mesh,
        in_specs=(
            P("tm", None, "space"),
            P("space", None, None, None),
            P(),
            P(),
            P(),
            P(),
            P(None, "space"),
            P("tm", "space"),
            P(None, "space"),
        ),
        out_specs=(P("tm", None, "space"), P("tm", "space")),
        check_vma=False,
    )
```

```python
import jax
import jax.numpy as jnp
from jax import lax
from jax.sharding import PartitionSpec as P

FINE = 2
SUB = 2
CG_ITERS = 8


def passed_along(value, axis, steps):
    count = lax.axis_size(axis)
    leading, last = (max(0, -steps), min(count, count - steps))
    return lax.ppermute(value, axis, [(source, source + steps) for source in range(leading, last)])


def shifted(value, axis, steps):
    count = lax.axis_size(axis)
    return lax.ppermute(value, axis, [(source, (source + steps) % count) for source in range(count)])


def exchange(partials, axis, down, up):
    count = lax.axis_size(axis)
    width = partials.shape[0]
    received = [partials]
    got_down = None
    got_up = None
    for steps in range(1, count):
        pieces = [partials]
        if steps == 1:
            pieces.append(down)
        if steps == count - 1:
            pieces.append(up)
        arrived = shifted(jnp.concatenate(pieces, axis=0), axis, steps)
        received.append(arrived[:width])
        offset = width
        if steps == 1:
            got_down = arrived[offset : offset + down.shape[0]]
            offset += down.shape[0]
        if steps == count - 1:
            got_up = arrived[offset : offset + up.shape[0]]
    while len(received) > 1 and len(received) % 2 == 0:
        half = len(received) // 2
        received = [received[k] + received[k + half] for k in range(half)]
    total = received[0]
    for extra in received[1:]:
        total = total + extra
    total = lax.optimization_barrier(
        jnp.broadcast_to(jnp.sum(total, axis=1, keepdims=True), total.shape)
    )
    return total, got_down, got_up


def ionic_update(voltage, gating, conductance, gate_center, gate_slope, gate_rate, reversal):
    for substep in range(SUB):
        steady = jax.nn.sigmoid((voltage[None, :] - gate_center) / gate_slope)
        damping = jnp.exp(-gate_rate * (0.5 + steady))
        gating = steady + (gating - steady) * damping
        current = jnp.sum(conductance * gating * (voltage[None, :] - reversal), axis=0)
        voltage = voltage - current
    return (voltage, gating)


def body(
    states_old,
    coupling,
    gate_center,
    gate_slope,
    gate_rate,
    reversal,
    conductance,
    stimulus,
    coarse_rate,
):
    num_blocks = coupling.shape[0]
    tile_width = coupling.shape[2]
    zero_rows = jnp.zeros((2, tile_width), jnp.float32)

    def couple_local(vector, upper_rows):
        extended = jnp.concatenate([vector, upper_rows], axis=0)
        ahead_sum = jnp.sum(
            coupling[:, 0] * extended[1 : num_blocks + 1, None, :]
            + coupling[:, 1] * extended[2 : num_blocks + 2, None, :],
            axis=-1,
        )
        carried = jnp.sum(coupling * vector[:, None, :, None], axis=2)
        inner = jnp.concatenate([zero_rows[:1], carried[:-1, 0]], axis=0) + jnp.concatenate(
            [zero_rows, carried[:-2, 1]], axis=0
        )
        spilled = jnp.stack([carried[-1, 0] + carried[-2, 1], carried[-1, 1]])
        return ahead_sum + inner, spilled

    def pad_head(rows):
        return jnp.concatenate(
            [rows, jnp.zeros((num_blocks - 2, tile_width), jnp.float32)], axis=0
        )

    space_count = lax.axis_size("space")
    on_last = lax.axis_index("space") == space_count - 1
    on_first = lax.axis_index("space") == 0

    def couple_part(vector, upper_rows):
        partial, spilled = couple_local(vector, upper_rows)
        return partial, jnp.where(on_last, jnp.zeros_like(spilled), spilled)

    ones = jnp.ones((num_blocks, tile_width), jnp.float32)
    local_degree, spilled = couple_part(ones, passed_along(ones[:2], "space", -1))
    degree = local_degree + pad_head(passed_along(spilled, "space", 1))

    def solve(right_side, side_steps=()):
        side_steps = list(side_steps)
        side_state = None
        upper = passed_along(right_side[:2], "space", -1)
        partial, spilled = couple_part(right_side, upper)
        local_mapped = right_side + degree * right_side - partial
        arrived = passed_along(spilled, "space", 1)
        mapped_up = passed_along(local_mapped[:2], "space", -1) - spilled
        residual = right_side - (local_mapped - pad_head(arrived))
        residual_up = upper - mapped_up
        iterate = right_side
        for iteration in range(CG_ITERS):
            partial, spilled = couple_part(residual, residual_up)
            local_image = residual + degree * residual - partial
            norm_part = jnp.sum(residual * residual, axis=0)
            energy_part = jnp.sum(residual * local_image, axis=0) - jnp.sum(
                residual_up * spilled, axis=0
            )
            sent_up = jnp.where(on_first, jnp.zeros_like(spilled), local_image[:2])
            sums, arrived, image_up = exchange(
                jnp.stack([norm_part, energy_part]), "space", spilled, sent_up
            )
            norm_now, energy = sums[0:1], sums[1:2]
            image = local_image - pad_head(arrived)
            image_up = image_up - spilled
            if iteration == 0:
                step_size = norm_now / energy
                direction, direction_up = residual, residual_up
                mapped, mapped_up = image, image_up
            else:
                ratio = norm_now / norm_before
                step_size = norm_now / (energy - ratio * norm_now / step_before)
                direction = residual + ratio * direction
                direction_up = residual_up + ratio * direction_up
                mapped = image + ratio * mapped
                mapped_up = image_up + ratio * mapped_up
            iterate = iterate + step_size * direction
            residual = residual - step_size * mapped
            residual_up = residual_up - step_size * mapped_up
            norm_before, step_before = norm_now, step_size
            if side_steps and iteration % 2 == 0:
                side_state = side_steps.pop(0)(side_state)
            if side_state is not None and iteration % 2 == 1:
                side_state, residual, residual_up, iterate = lax.optimization_barrier(
                    (side_state, residual, residual_up, iterate)
                )
        for step in side_steps:
            side_state = step(side_state)
        return iterate, side_state

    slices = lax.axis_size("tm")
    assert slices & (slices - 1) == 0

    def scan_steps(rows, rates, exponent):
        def first(_):
            return shifted(jnp.concatenate([exponent[None, :], rows], axis=0), "tm", 1)

        def doubling(span):
            def step(packed):
                earlier = shifted(packed, "tm", span)
                decay = jnp.exp(-rates * packed[0][None, :])
                return jnp.concatenate(
                    [(packed[0] + earlier[0])[None, :], decay * earlier[1:] + packed[1:]],
                    axis=0,
                )

            return step

        steps = [first]
        span = 1
        while span < slices:
            steps.append(doubling(span))
            span *= 2
        return steps

    def cyclic_scan(rows, rates, exponent):
        packed = None
        for step in scan_steps(rows, rates, exponent):
            packed = step(packed)
        return packed[1:], packed[0]

    exponent = 1.0 + jax.nn.sigmoid(states_old[0, 0])
    factor = jnp.exp(-coarse_rate * exponent[None, :])

    voltage = states_old[0, 0]
    gating = states_old[0, 1:]
    for fine_step in range(FINE):
        voltage, gating = ionic_update(
            voltage, gating, conductance, gate_center, gate_slope, gate_rate, reversal
        )
        side_steps = ()
        if fine_step == FINE - 1:
            side_steps = scan_steps(
                gating - factor[1:] * states_old[0, 1:], coarse_rate[1:], exponent
            )
        voltage = voltage + stimulus[0]
        voltage, gating_scan = solve(voltage.reshape(num_blocks, tile_width), side_steps)
        voltage = voltage.reshape(-1)
    gating_rows = gating_scan[1:]
    voltage_offset = voltage - factor[0] * states_old[0, 0]
    voltage_row, total_exponent = cyclic_scan(voltage_offset[None, :], coarse_rate[:1], exponent)
    loop_a = jnp.exp(-coarse_rate * total_exponent[None, :])
    new_state = jnp.concatenate([voltage_row, gating_rows], axis=0) / (1.0 - loop_a)
    return (new_state[None], new_state[0][None])


def solution(mesh):
    return jax.shard_map(
        body,
        mesh=mesh,
        in_specs=(
            P("tm", None, "space"),
            P("space", None, None, None),
            P(),
            P(),
            P(),
            P(),
            P(None, "space"),
            P("tm", "space"),
            P(None, "space"),
        ),
        out_specs=(P("tm", None, "space"), P("tm", "space")),
        check_vma=False,
    )
```

```python
import jax
import jax.numpy as jnp
from jax import lax
from jax.sharding import PartitionSpec as P

FINE = 2
SUB = 2
CG_ITERS = 8


def passed_along(value, axis, steps):
    count = lax.axis_size(axis)
    leading, last = (max(0, -steps), min(count, count - steps))
    return lax.ppermute(value, axis, [(source, source + steps) for source in range(leading, last)])


def shifted(value, axis, steps):
    count = lax.axis_size(axis)
    return lax.ppermute(value, axis, [(source, (source + steps) % count) for source in range(count)])


def exchange(partials, axis, down, up):
    count = lax.axis_size(axis)
    width = partials.shape[0]
    received = [partials]
    got_down = None
    got_up = None
    for steps in range(1, count):
        pieces = [partials]
        if steps == 1:
            pieces.append(down)
        if steps == count - 1:
            pieces.append(up)
        arrived = shifted(jnp.concatenate(pieces, axis=0), axis, steps)
        received.append(arrived[:width])
        offset = width
        if steps == 1:
            got_down = arrived[offset : offset + down.shape[0]]
            offset += down.shape[0]
        if steps == count - 1:
            got_up = arrived[offset : offset + up.shape[0]]
    while len(received) > 1 and len(received) % 2 == 0:
        half = len(received) // 2
        received = [received[k] + received[k + half] for k in range(half)]
    total = received[0]
    for extra in received[1:]:
        total = total + extra
    total = lax.optimization_barrier(
        jnp.broadcast_to(jnp.sum(total, axis=1, keepdims=True), total.shape)
    )
    return total, got_down, got_up


def ionic_update(voltage, gating, conductance, gate_center, gate_slope, gate_rate, reversal):
    for substep in range(SUB):
        steady = jax.nn.sigmoid((voltage[None, :] - gate_center) / gate_slope)
        damping = jnp.exp(-gate_rate * (0.5 + steady))
        gating = steady + (gating - steady) * damping
        current = jnp.sum(conductance * gating * (voltage[None, :] - reversal), axis=0)
        voltage = voltage - current
    return (voltage, gating)


def body(
    states_old,
    coupling,
    gate_center,
    gate_slope,
    gate_rate,
    reversal,
    conductance,
    stimulus,
    coarse_rate,
):
    num_blocks = coupling.shape[0]
    tile_width = coupling.shape[2]
    zero_rows = jnp.zeros((2, tile_width), jnp.float32)

    def couple_local(vector, upper_rows):
        extended = jnp.concatenate([vector, upper_rows], axis=0)
        ahead_sum = jnp.sum(
            coupling[:, 0] * extended[1 : num_blocks + 1, None, :]
            + coupling[:, 1] * extended[2 : num_blocks + 2, None, :],
            axis=-1,
        )
        carried = jnp.sum(coupling * vector[:, None, :, None], axis=2)
        inner = jnp.concatenate([zero_rows[:1], carried[:-1, 0]], axis=0) + jnp.concatenate(
            [zero_rows, carried[:-2, 1]], axis=0
        )
        spilled = jnp.stack([carried[-1, 0] + carried[-2, 1], carried[-1, 1]])
        return ahead_sum + inner, spilled

    def pad_head(rows):
        return jnp.concatenate(
            [rows, jnp.zeros((num_blocks - 2, tile_width), jnp.float32)], axis=0
        )

    space_count = lax.axis_size("space")
    on_last = lax.axis_index("space") == space_count - 1
    on_first = lax.axis_index("space") == 0

    def couple_part(vector, upper_rows):
        partial, spilled = couple_local(vector, upper_rows)
        return partial, jnp.where(on_last, jnp.zeros_like(spilled), spilled)

    ones = jnp.ones((num_blocks, tile_width), jnp.float32)
    local_degree, spilled = couple_part(ones, passed_along(ones[:2], "space", -1))
    degree = local_degree + pad_head(passed_along(spilled, "space", 1))

    def solve(right_side, side_steps=()):
        side_steps = list(side_steps)
        side_state = side_steps.pop(0)(None) if side_steps else None
        upper = passed_along(right_side[:2], "space", -1)
        partial, spilled = couple_part(right_side, upper)
        local_mapped = right_side + degree * right_side - partial
        arrived = passed_along(spilled, "space", 1)
        mapped_up = passed_along(local_mapped[:2], "space", -1) - spilled
        residual = right_side - (local_mapped - pad_head(arrived))
        residual_up = upper - mapped_up
        iterate = right_side
        for iteration in range(CG_ITERS):
            partial, spilled = couple_part(residual, residual_up)
            local_image = residual + degree * residual - partial
            norm_part = jnp.sum(residual * residual, axis=0)
            energy_part = jnp.sum(residual * local_image, axis=0) - jnp.sum(
                residual_up * spilled, axis=0
            )
            sent_up = jnp.where(on_first, jnp.zeros_like(spilled), local_image[:2])
            sums, arrived, image_up = exchange(
                jnp.stack([norm_part, energy_part]), "space", spilled, sent_up
            )
            norm_now, energy = sums[0:1], sums[1:2]
            image = local_image - pad_head(arrived)
            image_up = image_up - spilled
            if iteration == 0:
                step_size = norm_now / energy
                direction, direction_up = residual, residual_up
                mapped, mapped_up = image, image_up
            else:
                ratio = norm_now / norm_before
                step_size = norm_now / (energy - ratio * norm_now / step_before)
                direction = residual + ratio * direction
                direction_up = residual_up + ratio * direction_up
                mapped = image + ratio * mapped
                mapped_up = image_up + ratio * mapped_up
            iterate = iterate + step_size * direction
            residual = residual - step_size * mapped
            residual_up = residual_up - step_size * mapped_up
            norm_before, step_before = norm_now, step_size
            if side_state is not None and iteration % 2 == 1:
                side_state, residual, residual_up, iterate = lax.optimization_barrier(
                    (side_state, residual, residual_up, iterate)
                )
                if side_steps:
                    side_state = side_steps.pop(0)(side_state)
        for step in side_steps:
            side_state = step(side_state)
        return iterate, side_state

    slices = lax.axis_size("tm")
    assert slices & (slices - 1) == 0

    def scan_steps(rows, rates, exponent):
        def first(_):
            return shifted(jnp.concatenate([exponent[None, :], rows], axis=0), "tm", 1)

        def doubling(span):
            def step(packed):
                earlier = shifted(packed, "tm", span)
                decay = jnp.exp(-rates * packed[0][None, :])
                return jnp.concatenate(
                    [(packed[0] + earlier[0])[None, :], decay * earlier[1:] + packed[1:]],
                    axis=0,
                )

            return step

        steps = [first]
        span = 1
        while span < slices:
            steps.append(doubling(span))
            span *= 2
        return steps

    def cyclic_scan(rows, rates, exponent):
        packed = None
        for step in scan_steps(rows, rates, exponent):
            packed = step(packed)
        return packed[1:], packed[0]

    exponent = 1.0 + jax.nn.sigmoid(states_old[0, 0])
    factor = jnp.exp(-coarse_rate * exponent[None, :])

    voltage = states_old[0, 0]
    gating = states_old[0, 1:]
    for fine_step in range(FINE):
        voltage, gating = ionic_update(
            voltage, gating, conductance, gate_center, gate_slope, gate_rate, reversal
        )
        side_steps = ()
        if fine_step == FINE - 1:
            side_steps = scan_steps(
                gating - factor[1:] * states_old[0, 1:], coarse_rate[1:], exponent
            )
        voltage = voltage + stimulus[0]
        voltage, gating_scan = solve(voltage.reshape(num_blocks, tile_width), side_steps)
        voltage = voltage.reshape(-1)
    gating_rows = gating_scan[1:]
    voltage_offset = voltage - factor[0] * states_old[0, 0]
    voltage_row, total_exponent = cyclic_scan(voltage_offset[None, :], coarse_rate[:1], exponent)
    loop_a = jnp.exp(-coarse_rate * total_exponent[None, :])
    new_state = jnp.concatenate([voltage_row, gating_rows], axis=0) / (1.0 - loop_a)
    return (new_state[None], new_state[0][None])


def solution(mesh):
    return jax.shard_map(
        body,
        mesh=mesh,
        in_specs=(
            P("tm", None, "space"),
            P("space", None, None, None),
            P(),
            P(),
            P(),
            P(),
            P(None, "space"),
            P("tm", "space"),
            P(None, "space"),
        ),
        out_specs=(P("tm", None, "space"), P("tm", "space")),
        check_vma=False,
    )
```

```python
import jax
import jax.numpy as jnp
from jax import lax
from jax.sharding import PartitionSpec as P

FINE = 2
SUB = 2
CG_ITERS = 8


def passed_along(value, axis, steps):
    count = lax.axis_size(axis)
    leading, last = (max(0, -steps), min(count, count - steps))
    return lax.ppermute(value, axis, [(source, source + steps) for source in range(leading, last)])


def shifted(value, axis, steps):
    count = lax.axis_size(axis)
    return lax.ppermute(value, axis, [(source, (source + steps) % count) for source in range(count)])


def exchange(partials, axis, down, up):
    count = lax.axis_size(axis)
    width = partials.shape[0]
    received = [partials]
    got_down = None
    got_up = None
    for steps in range(1, count):
        pieces = [partials]
        if steps == 1:
            pieces.append(down)
        if steps == count - 1:
            pieces.append(up)
        arrived = shifted(jnp.concatenate(pieces, axis=0), axis, steps)
        received.append(arrived[:width])
        offset = width
        if steps == 1:
            got_down = arrived[offset : offset + down.shape[0]]
            offset += down.shape[0]
        if steps == count - 1:
            got_up = arrived[offset : offset + up.shape[0]]
    while len(received) > 1 and len(received) % 2 == 0:
        half = len(received) // 2
        received = [received[k] + received[k + half] for k in range(half)]
    total = received[0]
    for extra in received[1:]:
        total = total + extra
    total = lax.optimization_barrier(
        jnp.broadcast_to(jnp.sum(total, axis=1, keepdims=True), total.shape)
    )
    return total, got_down, got_up


def ionic_update(voltage, gating, conductance, gate_center, gate_slope, gate_rate, reversal):
    for substep in range(SUB):
        steady = jax.nn.sigmoid((voltage[None, :] - gate_center) / gate_slope)
        damping = jnp.exp(-gate_rate * (0.5 + steady))
        gating = steady + (gating - steady) * damping
        current = jnp.sum(conductance * gating * (voltage[None, :] - reversal), axis=0)
        voltage = voltage - current
    return (voltage, gating)


def body(
    states_old,
    coupling,
    gate_center,
    gate_slope,
    gate_rate,
    reversal,
    conductance,
    stimulus,
    coarse_rate,
):
    num_blocks = coupling.shape[0]
    tile_width = coupling.shape[2]
    zero_rows = jnp.zeros((2, tile_width), jnp.float32)

    def couple_local(vector, upper_rows):
        extended = jnp.concatenate([vector, upper_rows], axis=0)
        ahead_sum = jnp.sum(
            coupling[:, 0] * extended[1 : num_blocks + 1, None, :]
            + coupling[:, 1] * extended[2 : num_blocks + 2, None, :],
            axis=-1,
        )
        carried = jnp.sum(coupling * vector[:, None, :, None], axis=2)
        inner = jnp.concatenate([zero_rows[:1], carried[:-1, 0]], axis=0) + jnp.concatenate(
            [zero_rows, carried[:-2, 1]], axis=0
        )
        spilled = jnp.stack([carried[-1, 0] + carried[-2, 1], carried[-1, 1]])
        return ahead_sum + inner, spilled

    def pad_head(rows):
        return jnp.concatenate(
            [rows, jnp.zeros((num_blocks - 2, tile_width), jnp.float32)], axis=0
        )

    space_count = lax.axis_size("space")
    on_last = lax.axis_index("space") == space_count - 1
    on_first = lax.axis_index("space") == 0

    def couple_part(vector, upper_rows):
        partial, spilled = couple_local(vector, upper_rows)
        return partial, jnp.where(on_last, jnp.zeros_like(spilled), spilled)

    ones = jnp.ones((num_blocks, tile_width), jnp.float32)
    local_degree, spilled = couple_part(ones, passed_along(ones[:2], "space", -1))
    degree = local_degree + pad_head(passed_along(spilled, "space", 1))

    def solve(right_side, side_steps=()):
        side_steps = list(side_steps)
        side_state = side_steps.pop(0)(None) if side_steps else None
        upper = passed_along(right_side[:2], "space", -1)
        partial, spilled = couple_part(right_side, upper)
        local_mapped = right_side + degree * right_side - partial
        arrived = passed_along(spilled, "space", 1)
        mapped_up = passed_along(local_mapped[:2], "space", -1) - spilled
        residual = right_side - (local_mapped - pad_head(arrived))
        residual_up = upper - mapped_up
        iterate = right_side
        for iteration in range(CG_ITERS):
            partial, spilled = couple_part(residual, residual_up)
            local_image = residual + degree * residual - partial
            norm_part = jnp.sum(residual * residual, axis=0)
            energy_part = jnp.sum(residual * local_image, axis=0) - jnp.sum(
                residual_up * spilled, axis=0
            )
            sent_up = jnp.where(on_first, jnp.zeros_like(spilled), local_image[:2])
            sums, arrived, image_up = exchange(
                jnp.stack([norm_part, energy_part]), "space", spilled, sent_up
            )
            norm_now, energy = sums[0:1], sums[1:2]
            image = local_image - pad_head(arrived)
            image_up = image_up - spilled
            if iteration == 0:
                step_size = norm_now / energy
                direction, direction_up = residual, residual_up
                mapped, mapped_up = image, image_up
            else:
                ratio = norm_now / norm_before
                step_size = norm_now / (energy - ratio * norm_now / step_before)
                direction = residual + ratio * direction
                direction_up = residual_up + ratio * direction_up
                mapped = image + ratio * mapped
                mapped_up = image_up + ratio * mapped_up
            iterate = iterate + step_size * direction
            residual = residual - step_size * mapped
            residual_up = residual_up - step_size * mapped_up
            norm_before, step_before = norm_now, step_size
            if side_state is not None and iteration % 2 == 1:
                side_state, residual, residual_up, iterate = lax.optimization_barrier(
                    (side_state, residual, residual_up, iterate)
                )
                if side_steps:
                    side_state = side_steps.pop(0)(side_state)
        for step in side_steps:
            side_state = step(side_state)
        return iterate, side_state

    slices = lax.axis_size("tm")
    assert slices & (slices - 1) == 0

    def scan_steps(rows, rates, exponent):
        def first(_):
            return shifted(jnp.concatenate([exponent[None, :], rows], axis=0), "tm", 1)

        def doubling(span):
            def step(packed):
                earlier = shifted(packed, "tm", span)
                decay = jnp.exp(-rates * packed[0][None, :])
                return jnp.concatenate(
                    [(packed[0] + earlier[0])[None, :], decay * earlier[1:] + packed[1:]],
                    axis=0,
                )

            return step

        steps = [first]
        span = 1
        while span < slices:
            steps.append(doubling(span))
            span *= 2
        return steps

    def paired(first_step, second_step):
        def step(state):
            if state is None:
                return first_step(None), second_step(None)
            return first_step(state[0]), second_step(state[1])

        return step

    def cyclic_scan(rows, rates, exponent):
        packed = None
        for step in scan_steps(rows, rates, exponent):
            packed = step(packed)
        return packed[1:], packed[0]

    exponent = 1.0 + jax.nn.sigmoid(states_old[0, 0])
    factor = jnp.exp(-coarse_rate * exponent[None, :])

    voltage = states_old[0, 0]
    gating = states_old[0, 1:]
    for fine_step in range(FINE):
        voltage, gating = ionic_update(
            voltage, gating, conductance, gate_center, gate_slope, gate_rate, reversal
        )
        side_steps = ()
        if fine_step == FINE - 1:
            gating_offset = gating - factor[1:] * states_old[0, 1:]
            half = gating_offset.shape[0] // 2
            side_steps = [
                paired(first_half, second_half)
                for first_half, second_half in zip(
                    scan_steps(gating_offset[:half], coarse_rate[1 : half + 1], exponent),
                    scan_steps(gating_offset[half:], coarse_rate[half + 1 :], exponent),
                )
            ]
        voltage = voltage + stimulus[0]
        voltage, gating_scan = solve(voltage.reshape(num_blocks, tile_width), side_steps)
        voltage = voltage.reshape(-1)
    gating_rows = jnp.concatenate([gating_scan[0][1:], gating_scan[1][1:]], axis=0)
    voltage_offset = voltage - factor[0] * states_old[0, 0]
    voltage_row, total_exponent = cyclic_scan(voltage_offset[None, :], coarse_rate[:1], exponent)
    loop_a = jnp.exp(-coarse_rate * total_exponent[None, :])
    new_state = jnp.concatenate([voltage_row, gating_rows], axis=0) / (1.0 - loop_a)
    return (new_state[None], new_state[0][None])


def solution(mesh):
    return jax.shard_map(
        body,
        mesh=mesh,
        in_specs=(
            P("tm", None, "space"),
            P("space", None, None, None),
            P(),
            P(),
            P(),
            P(),
            P(None, "space"),
            P("tm", "space"),
            P(None, "space"),
        ),
        out_specs=(P("tm", None, "space"), P("tm", "space")),
        check_vma=False,
    )
```

```python
import jax
import jax.numpy as jnp
from jax import lax
from jax.sharding import PartitionSpec as P

FINE = 2
SUB = 2
CG_ITERS = 8


def passed_along(value, axis, steps):
    count = lax.axis_size(axis)
    leading, last = (max(0, -steps), min(count, count - steps))
    return lax.ppermute(value, axis, [(source, source + steps) for source in range(leading, last)])


def shifted(value, axis, steps):
    count = lax.axis_size(axis)
    return lax.ppermute(value, axis, [(source, (source + steps) % count) for source in range(count)])


def exchange(partials, axis, down, up):
    count = lax.axis_size(axis)
    width = partials.shape[0]
    received = [partials]
    got_down = None
    got_up = None
    for steps in range(1, count):
        pieces = [partials]
        if steps == 1:
            pieces.append(down)
        if steps == count - 1:
            pieces.append(up)
        arrived = shifted(jnp.concatenate(pieces, axis=0), axis, steps)
        received.append(arrived[:width])
        offset = width
        if steps == 1:
            got_down = arrived[offset : offset + down.shape[0]]
            offset += down.shape[0]
        if steps == count - 1:
            got_up = arrived[offset : offset + up.shape[0]]
    while len(received) > 1 and len(received) % 2 == 0:
        half = len(received) // 2
        received = [received[k] + received[k + half] for k in range(half)]
    total = received[0]
    for extra in received[1:]:
        total = total + extra
    total = lax.optimization_barrier(
        jnp.broadcast_to(jnp.sum(total, axis=1, keepdims=True), total.shape)
    )
    return total, got_down, got_up


def ionic_update(voltage, gating, conductance, gate_center, gate_slope, gate_rate, reversal):
    for substep in range(SUB):
        steady = jax.nn.sigmoid((voltage[None, :] - gate_center) / gate_slope)
        damping = jnp.exp(-gate_rate * (0.5 + steady))
        gating = steady + (gating - steady) * damping
        current = jnp.sum(conductance * gating * (voltage[None, :] - reversal), axis=0)
        voltage = voltage - current
    return (voltage, gating)


def body(
    states_old,
    coupling,
    gate_center,
    gate_slope,
    gate_rate,
    reversal,
    conductance,
    stimulus,
    coarse_rate,
):
    num_blocks = coupling.shape[0]
    tile_width = coupling.shape[2]
    zero_rows = jnp.zeros((2, tile_width), jnp.float32)

    def couple_local(vector, upper_rows):
        extended = jnp.concatenate([vector, upper_rows], axis=0)
        ahead_sum = jnp.sum(
            coupling[:, 0] * extended[1 : num_blocks + 1, None, :]
            + coupling[:, 1] * extended[2 : num_blocks + 2, None, :],
            axis=-1,
        )
        carried = jnp.sum(coupling * vector[:, None, :, None], axis=2)
        inner = jnp.concatenate([zero_rows[:1], carried[:-1, 0]], axis=0) + jnp.concatenate(
            [zero_rows, carried[:-2, 1]], axis=0
        )
        spilled = jnp.stack([carried[-1, 0] + carried[-2, 1], carried[-1, 1]])
        return ahead_sum + inner, spilled

    def pad_head(rows):
        return jnp.concatenate(
            [rows, jnp.zeros((num_blocks - 2, tile_width), jnp.float32)], axis=0
        )

    space_count = lax.axis_size("space")
    on_last = lax.axis_index("space") == space_count - 1
    on_first = lax.axis_index("space") == 0

    def couple_part(vector, upper_rows):
        partial, spilled = couple_local(vector, upper_rows)
        return partial, jnp.where(on_last, jnp.zeros_like(spilled), spilled)

    ones = jnp.ones((num_blocks, tile_width), jnp.float32)
    local_degree, spilled = couple_part(ones, passed_along(ones[:2], "space", -1))
    degree = local_degree + pad_head(passed_along(spilled, "space", 1))

    def solve(right_side, side_steps=()):
        side_steps = list(side_steps)
        side_state = side_steps.pop(0)(None) if side_steps else None
        upper = passed_along(right_side[:2], "space", -1)
        partial, spilled = couple_part(right_side, upper)
        local_mapped = right_side + degree * right_side - partial
        arrived = passed_along(spilled, "space", 1)
        mapped_up = passed_along(local_mapped[:2], "space", -1) - spilled
        residual = right_side - (local_mapped - pad_head(arrived))
        residual_up = upper - mapped_up
        iterate = right_side
        for iteration in range(CG_ITERS):
            partial, spilled = couple_part(residual, residual_up)
            local_image = residual + degree * residual - partial
            norm_part = jnp.sum(residual * residual, axis=0)
            energy_part = jnp.sum(residual * local_image, axis=0) - jnp.sum(
                residual_up * spilled, axis=0
            )
            sent_up = jnp.where(on_first, jnp.zeros_like(spilled), local_image[:2])
            sums, arrived, image_up = exchange(
                jnp.stack([norm_part, energy_part]), "space", spilled, sent_up
            )
            norm_now, energy = sums[0:1], sums[1:2]
            image = local_image - pad_head(arrived)
            image_up = image_up - spilled
            if iteration == 0:
                step_size = norm_now / energy
                direction, direction_up = residual, residual_up
                mapped, mapped_up = image, image_up
            else:
                ratio = norm_now / norm_before
                step_size = norm_now / (energy - ratio * norm_now / step_before)
                direction = residual + ratio * direction
                direction_up = residual_up + ratio * direction_up
                mapped = image + ratio * mapped
                mapped_up = image_up + ratio * mapped_up
            iterate = iterate + step_size * direction
            residual = residual - step_size * mapped
            residual_up = residual_up - step_size * mapped_up
            norm_before, step_before = norm_now, step_size
            if side_state is not None and iteration in (0, 1, 4, CG_ITERS - 1):
                side_state, residual, residual_up, iterate = lax.optimization_barrier(
                    (side_state, residual, residual_up, iterate)
                )
                if side_steps:
                    side_state = side_steps.pop(0)(side_state)
        for step in side_steps:
            side_state = step(side_state)
        return iterate, side_state

    slices = lax.axis_size("tm")
    assert slices & (slices - 1) == 0

    def scan_steps(rows, rates, exponent):
        def first(_):
            return shifted(jnp.concatenate([exponent[None, :], rows], axis=0), "tm", 1)

        def doubling(span):
            def step(packed):
                earlier = shifted(packed, "tm", span)
                decay = jnp.exp(-rates * packed[0][None, :])
                return jnp.concatenate(
                    [(packed[0] + earlier[0])[None, :], decay * earlier[1:] + packed[1:]],
                    axis=0,
                )

            return step

        steps = [first]
        span = 1
        while span < slices:
            steps.append(doubling(span))
            span *= 2
        return steps

    def cyclic_scan(rows, rates, exponent):
        packed = None
        for step in scan_steps(rows, rates, exponent):
            packed = step(packed)
        return packed[1:], packed[0]

    exponent = 1.0 + jax.nn.sigmoid(states_old[0, 0])
    factor = jnp.exp(-coarse_rate * exponent[None, :])

    voltage = states_old[0, 0]
    gating = states_old[0, 1:]
    for fine_step in range(FINE):
        voltage, gating = ionic_update(
            voltage, gating, conductance, gate_center, gate_slope, gate_rate, reversal
        )
        side_steps = ()
        if fine_step == FINE - 1:
            side_steps = scan_steps(
                gating - factor[1:] * states_old[0, 1:], coarse_rate[1:], exponent
            )
        voltage = voltage + stimulus[0]
        voltage, gating_scan = solve(voltage.reshape(num_blocks, tile_width), side_steps)
        voltage = voltage.reshape(-1)
    gating_rows = gating_scan[1:]
    voltage_offset = voltage - factor[0] * states_old[0, 0]
    voltage_row, total_exponent = cyclic_scan(voltage_offset[None, :], coarse_rate[:1], exponent)
    loop_a = jnp.exp(-coarse_rate * total_exponent[None, :])
    new_state = jnp.concatenate([voltage_row, gating_rows], axis=0) / (1.0 - loop_a)
    return (new_state[None], new_state[0][None])


def solution(mesh):
    return jax.shard_map(
        body,
        mesh=mesh,
        in_specs=(
            P("tm", None, "space"),
            P("space", None, None, None),
            P(),
            P(),
            P(),
            P(),
            P(None, "space"),
            P("tm", "space"),
            P(None, "space"),
        ),
        out_specs=(P("tm", None, "space"), P("tm", "space")),
        check_vma=False,
    )
```

```python
import jax
import jax.numpy as jnp
from jax import lax
from jax.sharding import PartitionSpec as P

FINE = 2
SUB = 2
CG_ITERS = 8


def passed_along(value, axis, steps):
    count = lax.axis_size(axis)
    leading, last = (max(0, -steps), min(count, count - steps))
    return lax.ppermute(value, axis, [(source, source + steps) for source in range(leading, last)])


def shifted(value, axis, steps):
    count = lax.axis_size(axis)
    return lax.ppermute(value, axis, [(source, (source + steps) % count) for source in range(count)])


def exchange(partials, axis, down, up):
    count = lax.axis_size(axis)
    width = partials.shape[0]
    received = [partials]
    got_down = None
    got_up = None
    for steps in range(1, count):
        pieces = [partials]
        if steps == 1:
            pieces.append(down)
        if steps == count - 1:
            pieces.append(up)
        arrived = shifted(jnp.concatenate(pieces, axis=0), axis, steps)
        received.append(arrived[:width])
        offset = width
        if steps == 1:
            got_down = arrived[offset : offset + down.shape[0]]
            offset += down.shape[0]
        if steps == count - 1:
            got_up = arrived[offset : offset + up.shape[0]]
    while len(received) > 1 and len(received) % 2 == 0:
        half = len(received) // 2
        received = [received[k] + received[k + half] for k in range(half)]
    total = received[0]
    for extra in received[1:]:
        total = total + extra
    total = lax.optimization_barrier(
        jnp.broadcast_to(jnp.sum(total, axis=1, keepdims=True), total.shape)
    )
    return total, got_down, got_up


def ionic_update(voltage, gating, conductance, gate_center, gate_slope, gate_rate, reversal):
    for substep in range(SUB):
        steady = jax.nn.sigmoid((voltage[None, :] - gate_center) / gate_slope)
        damping = jnp.exp(-gate_rate * (0.5 + steady))
        gating = steady + (gating - steady) * damping
        current = jnp.sum(conductance * gating * (voltage[None, :] - reversal), axis=0)
        voltage = voltage - current
    return (voltage, gating)


def body(
    states_old,
    coupling,
    gate_center,
    gate_slope,
    gate_rate,
    reversal,
    conductance,
    stimulus,
    coarse_rate,
):
    num_blocks = coupling.shape[0]
    tile_width = coupling.shape[2]
    zero_rows = jnp.zeros((2, tile_width), jnp.float32)

    def couple_local(vector, upper_rows):
        extended = jnp.concatenate([vector, upper_rows], axis=0)
        ahead_sum = jnp.sum(
            coupling[:, 0] * extended[1 : num_blocks + 1, None, :]
            + coupling[:, 1] * extended[2 : num_blocks + 2, None, :],
            axis=-1,
        )
        carried = jnp.sum(coupling * vector[:, None, :, None], axis=2)
        inner = jnp.concatenate([zero_rows[:1], carried[:-1, 0]], axis=0) + jnp.concatenate(
            [zero_rows, carried[:-2, 1]], axis=0
        )
        spilled = jnp.stack([carried[-1, 0] + carried[-2, 1], carried[-1, 1]])
        return ahead_sum + inner, spilled

    def pad_head(rows):
        return jnp.concatenate(
            [rows, jnp.zeros((num_blocks - 2, tile_width), jnp.float32)], axis=0
        )

    space_count = lax.axis_size("space")
    on_last = lax.axis_index("space") == space_count - 1
    on_first = lax.axis_index("space") == 0

    def couple_part(vector, upper_rows):
        partial, spilled = couple_local(vector, upper_rows)
        return partial, jnp.where(on_last, jnp.zeros_like(spilled), spilled)

    ones = jnp.ones((num_blocks, tile_width), jnp.float32)
    local_degree, spilled = couple_part(ones, passed_along(ones[:2], "space", -1))
    degree = local_degree + pad_head(passed_along(spilled, "space", 1))

    def solve(right_side, side_steps=()):
        side_steps = list(side_steps)
        side_state = side_steps.pop(0)(None) if side_steps else None
        upper = passed_along(right_side[:2], "space", -1)
        partial, spilled = couple_part(right_side, upper)
        local_mapped = right_side + degree * right_side - partial
        arrived = passed_along(spilled, "space", 1)
        mapped_up = passed_along(local_mapped[:2], "space", -1) - spilled
        residual = right_side - (local_mapped - pad_head(arrived))
        residual_up = upper - mapped_up
        iterate = right_side
        for iteration in range(CG_ITERS):
            partial, spilled = couple_part(residual, residual_up)
            local_image = residual + degree * residual - partial
            norm_part = jnp.sum(residual * residual, axis=0)
            energy_part = jnp.sum(residual * local_image, axis=0) - jnp.sum(
                residual_up * spilled, axis=0
            )
            sent_up = jnp.where(on_first, jnp.zeros_like(spilled), local_image[:2])
            sums, arrived, image_up = exchange(
                jnp.stack([norm_part, energy_part]), "space", spilled, sent_up
            )
            norm_now, energy = sums[0:1], sums[1:2]
            image = local_image - pad_head(arrived)
            image_up = image_up - spilled
            if iteration == 0:
                step_size = norm_now / energy
                direction, direction_up = residual, residual_up
                mapped, mapped_up = image, image_up
            else:
                ratio = norm_now / norm_before
                step_size = norm_now / (energy - ratio * norm_now / step_before)
                direction = residual + ratio * direction
                direction_up = residual_up + ratio * direction_up
                mapped = image + ratio * mapped
                mapped_up = image_up + ratio * mapped_up
            iterate = iterate + step_size * direction
            residual = residual - step_size * mapped
            residual_up = residual_up - step_size * mapped_up
            norm_before, step_before = norm_now, step_size
            if side_state is not None and iteration in (0, 1, 4, CG_ITERS - 1):
                side_state, residual, residual_up, iterate = lax.optimization_barrier(
                    (side_state, residual, residual_up, iterate)
                )
                if side_steps:
                    side_state = side_steps.pop(0)(side_state)
        for step in side_steps:
            side_state = step(side_state)
        return iterate, side_state

    slices = lax.axis_size("tm")
    assert slices & (slices - 1) == 0

    def scan_steps(rows, rates, exponent):
        def first(_):
            return shifted(jnp.concatenate([exponent[None, :], rows], axis=0), "tm", 1)

        def doubling(span):
            def step(packed):
                earlier = shifted(packed, "tm", span)
                decay = jnp.exp(-rates * packed[0][None, :])
                return jnp.concatenate(
                    [(packed[0] + earlier[0])[None, :], decay * earlier[1:] + packed[1:]],
                    axis=0,
                )

            return step

        steps = [first]
        span = 1
        while span < slices:
            steps.append(doubling(span))
            span *= 2
        return steps

    def transposed_loop(rows, rates, exponent):
        width = rows.shape[1] // slices
        packed = jnp.concatenate([exponent[None, :], rows], axis=0)
        packed = packed.reshape(rows.shape[0] + 1, slices, width).transpose(1, 0, 2)
        gathered = lax.all_to_all(packed, "tm", 0, 0)
        mine = lax.axis_index("tm")
        local_rates = lax.dynamic_slice_in_dim(rates, mine * width, width, axis=1)
        factors = [jnp.exp(-local_rates * gathered[k, 0][None, :]) for k in range(slices)]
        offsets = [gathered[k, 1:] for k in range(slices)]
        loop_a = jnp.ones_like(factors[0])
        loop_r = jnp.zeros_like(offsets[0])
        for k in range(slices):
            loop_a = factors[k] * loop_a
            loop_r = factors[k] * loop_r + offsets[k]
        current = loop_r / (1.0 - loop_a)
        results = []
        for k in range(slices):
            results.append(current)
            current = factors[k] * current + offsets[k]
        returned = lax.all_to_all(jnp.stack(results), "tm", 0, 0)
        return returned.transpose(1, 0, 2).reshape(rows.shape)

    def cyclic_scan(rows, rates, exponent):
        packed = None
        for step in scan_steps(rows, rates, exponent):
            packed = step(packed)
        return packed[1:], packed[0]

    exponent = 1.0 + jax.nn.sigmoid(states_old[0, 0])
    factor = jnp.exp(-coarse_rate * exponent[None, :])

    voltage = states_old[0, 0]
    gating = states_old[0, 1:]
    for fine_step in range(FINE):
        voltage, gating = ionic_update(
            voltage, gating, conductance, gate_center, gate_slope, gate_rate, reversal
        )
        side_steps = ()
        if fine_step == FINE - 1:
            gating_rows = transposed_loop(
                gating - factor[1:] * states_old[0, 1:], coarse_rate[1:], exponent
            )
        voltage = voltage + stimulus[0]
        voltage, gating_scan = solve(voltage.reshape(num_blocks, tile_width), side_steps)
        voltage = voltage.reshape(-1)
    voltage_offset = voltage - factor[0] * states_old[0, 0]
    voltage_row, total_exponent = cyclic_scan(voltage_offset[None, :], coarse_rate[:1], exponent)
    loop_a = jnp.exp(-coarse_rate * total_exponent[None, :])
    new_state = jnp.concatenate([voltage_row / (1.0 - loop_a[:1]), gating_rows], axis=0)
    return (new_state[None], new_state[0][None])


def solution(mesh):
    return jax.shard_map(
        body,
        mesh=mesh,
        in_specs=(
            P("tm", None, "space"),
            P("space", None, None, None),
            P(),
            P(),
            P(),
            P(),
            P(None, "space"),
            P("tm", "space"),
            P(None, "space"),
        ),
        out_specs=(P("tm", None, "space"), P("tm", "space")),
        check_vma=False,
    )
```

```python
import jax
import jax.numpy as jnp
from jax import lax
from jax.sharding import PartitionSpec as P

FINE = 2
SUB = 2
CG_ITERS = 8


def passed_along(value, axis, steps):
    count = lax.axis_size(axis)
    leading, last = (max(0, -steps), min(count, count - steps))
    return lax.ppermute(value, axis, [(source, source + steps) for source in range(leading, last)])


def shifted(value, axis, steps):
    count = lax.axis_size(axis)
    return lax.ppermute(value, axis, [(source, (source + steps) % count) for source in range(count)])


def exchange(partials, axis, down, up):
    count = lax.axis_size(axis)
    width = partials.shape[0]
    received = [partials]
    got_down = None
    got_up = None
    for steps in range(1, count):
        pieces = [partials]
        if steps == 1:
            pieces.append(down)
        if steps == count - 1:
            pieces.append(up)
        arrived = shifted(jnp.concatenate(pieces, axis=0), axis, steps)
        received.append(arrived[:width])
        offset = width
        if steps == 1:
            got_down = arrived[offset : offset + down.shape[0]]
            offset += down.shape[0]
        if steps == count - 1:
            got_up = arrived[offset : offset + up.shape[0]]
    while len(received) > 1 and len(received) % 2 == 0:
        half = len(received) // 2
        received = [received[k] + received[k + half] for k in range(half)]
    total = received[0]
    for extra in received[1:]:
        total = total + extra
    total = lax.optimization_barrier(
        jnp.broadcast_to(jnp.sum(total, axis=1, keepdims=True), total.shape)
    )
    return total, got_down, got_up


def ionic_update(voltage, gating, conductance, gate_center, gate_slope, gate_rate, reversal):
    for substep in range(SUB):
        steady = jax.nn.sigmoid((voltage[None, :] - gate_center) / gate_slope)
        damping = jnp.exp(-gate_rate * (0.5 + steady))
        gating = steady + (gating - steady) * damping
        current = jnp.sum(conductance * gating * (voltage[None, :] - reversal), axis=0)
        voltage = voltage - current
    return (voltage, gating)


def body(
    states_old,
    coupling,
    gate_center,
    gate_slope,
    gate_rate,
    reversal,
    conductance,
    stimulus,
    coarse_rate,
):
    num_blocks = coupling.shape[0]
    tile_width = coupling.shape[2]
    zero_rows = jnp.zeros((2, tile_width), jnp.float32)

    def couple_local(vector, upper_rows):
        extended = jnp.concatenate([vector, upper_rows], axis=0)
        ahead_sum = jnp.sum(
            coupling[:, 0] * extended[1 : num_blocks + 1, None, :]
            + coupling[:, 1] * extended[2 : num_blocks + 2, None, :],
            axis=-1,
        )
        carried = jnp.sum(coupling * vector[:, None, :, None], axis=2)
        inner = jnp.concatenate([zero_rows[:1], carried[:-1, 0]], axis=0) + jnp.concatenate(
            [zero_rows, carried[:-2, 1]], axis=0
        )
        spilled = jnp.stack([carried[-1, 0] + carried[-2, 1], carried[-1, 1]])
        return ahead_sum + inner, spilled

    def pad_head(rows):
        return jnp.concatenate(
            [rows, jnp.zeros((num_blocks - 2, tile_width), jnp.float32)], axis=0
        )

    space_count = lax.axis_size("space")
    on_last = lax.axis_index("space") == space_count - 1
    on_first = lax.axis_index("space") == 0

    def couple_part(vector, upper_rows):
        partial, spilled = couple_local(vector, upper_rows)
        return partial, jnp.where(on_last, jnp.zeros_like(spilled), spilled)

    ones = jnp.ones((num_blocks, tile_width), jnp.float32)
    local_degree, spilled = couple_part(ones, passed_along(ones[:2], "space", -1))
    degree = local_degree + pad_head(passed_along(spilled, "space", 1))

    def solve(right_side, side_steps=()):
        side_steps = list(side_steps)
        side_state = side_steps.pop(0)(None) if side_steps else None
        upper = passed_along(right_side[:2], "space", -1)
        partial, spilled = couple_part(right_side, upper)
        local_mapped = right_side + degree * right_side - partial
        arrived = passed_along(spilled, "space", 1)
        mapped_up = passed_along(local_mapped[:2], "space", -1) - spilled
        residual = right_side - (local_mapped - pad_head(arrived))
        residual_up = upper - mapped_up
        iterate = right_side
        for iteration in range(CG_ITERS):
            partial, spilled = couple_part(residual, residual_up)
            local_image = residual + degree * residual - partial
            norm_part = jnp.sum(residual * residual, axis=0)
            energy_part = jnp.sum(residual * local_image, axis=0) - jnp.sum(
                residual_up * spilled, axis=0
            )
            sent_up = jnp.where(on_first, jnp.zeros_like(spilled), local_image[:2])
            sums, arrived, image_up = exchange(
                jnp.stack([norm_part, energy_part]), "space", spilled, sent_up
            )
            norm_now, energy = sums[0:1], sums[1:2]
            image = local_image - pad_head(arrived)
            image_up = image_up - spilled
            if iteration == 0:
                step_size = norm_now / energy
                direction, direction_up = residual, residual_up
                mapped, mapped_up = image, image_up
            else:
                ratio = norm_now / norm_before
                step_size = norm_now / (energy - ratio * norm_now / step_before)
                direction = residual + ratio * direction
                direction_up = residual_up + ratio * direction_up
                mapped = image + ratio * mapped
                mapped_up = image_up + ratio * mapped_up
            iterate = iterate + step_size * direction
            residual = residual - step_size * mapped
            residual_up = residual_up - step_size * mapped_up
            norm_before, step_before = norm_now, step_size
            if side_state is not None and iteration in (0, 1, 4, CG_ITERS - 1):
                side_state, residual, residual_up, iterate = lax.optimization_barrier(
                    (side_state, residual, residual_up, iterate)
                )
                if side_steps:
                    side_state = side_steps.pop(0)(side_state)
        for step in side_steps:
            side_state = step(side_state)
        return iterate, side_state

    slices = lax.axis_size("tm")
    assert slices & (slices - 1) == 0

    def scan_steps(rows, rates, exponent):
        def first(_):
            return shifted(jnp.concatenate([exponent[None, :], rows], axis=0), "tm", 1)

        def doubling(span):
            def step(packed):
                earlier = shifted(packed, "tm", span)
                decay = jnp.exp(-rates * packed[0][None, :])
                return jnp.concatenate(
                    [(packed[0] + earlier[0])[None, :], decay * earlier[1:] + packed[1:]],
                    axis=0,
                )

            return step

        steps = [first]
        span = 1
        while span < slices:
            steps.append(doubling(span))
            span *= 2
        return steps

    def transposed_loop(rows, rates, exponent):
        width = rows.shape[1] // slices
        packed = jnp.concatenate([exponent[None, :], rows], axis=0)
        packed = packed.reshape(rows.shape[0] + 1, slices, width).transpose(1, 0, 2)
        gathered = lax.all_to_all(packed, "tm", 0, 0)
        mine = lax.axis_index("tm")
        local_rates = lax.dynamic_slice_in_dim(rates, mine * width, width, axis=1)
        factors = [jnp.exp(-local_rates * gathered[k, 0][None, :]) for k in range(slices)]
        offsets = [gathered[k, 1:] for k in range(slices)]
        loop_a = jnp.ones_like(factors[0])
        loop_r = jnp.zeros_like(offsets[0])
        for k in range(slices):
            loop_a = factors[k] * loop_a
            loop_r = factors[k] * loop_r + offsets[k]
        current = loop_r / (1.0 - loop_a)
        results = []
        for k in range(slices):
            results.append(current)
            current = factors[k] * current + offsets[k]
        returned = lax.all_to_all(jnp.stack(results), "tm", 0, 0)
        return returned.transpose(1, 0, 2).reshape(rows.shape)

    def cyclic_scan(rows, rates, exponent):
        packed = None
        for step in scan_steps(rows, rates, exponent):
            packed = step(packed)
        return packed[1:], packed[0]

    exponent = 1.0 + jax.nn.sigmoid(states_old[0, 0])
    factor = jnp.exp(-coarse_rate * exponent[None, :])

    voltage = states_old[0, 0]
    gating = states_old[0, 1:]
    for fine_step in range(FINE):
        voltage, gating = ionic_update(
            voltage, gating, conductance, gate_center, gate_slope, gate_rate, reversal
        )
        side_steps = ()
        if fine_step == FINE - 1:
            side_steps = scan_steps(
                gating - factor[1:] * states_old[0, 1:], coarse_rate[1:], exponent
            )
        voltage = voltage + stimulus[0]
        voltage, gating_scan = solve(voltage.reshape(num_blocks, tile_width), side_steps)
        voltage = voltage.reshape(-1)
    gating_rows = gating_scan[1:]
    voltage_offset = voltage - factor[0] * states_old[0, 0]
    voltage_row = transposed_loop(voltage_offset[None, :], coarse_rate[:1], exponent)
    loop_a = jnp.exp(-coarse_rate[1:] * gating_scan[0][None, :])
    new_state = jnp.concatenate([voltage_row, gating_rows / (1.0 - loop_a)], axis=0)
    return (new_state[None], new_state[0][None])


def solution(mesh):
    return jax.shard_map(
        body,
        mesh=mesh,
        in_specs=(
            P("tm", None, "space"),
            P("space", None, None, None),
            P(),
            P(),
            P(),
            P(),
            P(None, "space"),
            P("tm", "space"),
            P(None, "space"),
        ),
        out_specs=(P("tm", None, "space"), P("tm", "space")),
        check_vma=False,
    )
```

```python
import jax
import jax.numpy as jnp
from jax import lax
from jax.sharding import PartitionSpec as P

FINE = 2
SUB = 2
CG_ITERS = 8


def passed_along(value, axis, steps):
    count = lax.axis_size(axis)
    leading, last = (max(0, -steps), min(count, count - steps))
    return lax.ppermute(value, axis, [(source, source + steps) for source in range(leading, last)])


def shifted(value, axis, steps):
    count = lax.axis_size(axis)
    return lax.ppermute(value, axis, [(source, (source + steps) % count) for source in range(count)])


def exchange(partials, axis, down, up):
    count = lax.axis_size(axis)
    width = partials.shape[0]
    received = [partials]
    got_down = None
    got_up = None
    for steps in range(1, count):
        pieces = [partials]
        if steps == 1:
            pieces.append(down)
        if steps == count - 1:
            pieces.append(up)
        arrived = shifted(jnp.concatenate(pieces, axis=0), axis, steps)
        received.append(arrived[:width])
        offset = width
        if steps == 1:
            got_down = arrived[offset : offset + down.shape[0]]
            offset += down.shape[0]
        if steps == count - 1:
            got_up = arrived[offset : offset + up.shape[0]]
    while len(received) > 1 and len(received) % 2 == 0:
        half = len(received) // 2
        received = [received[k] + received[k + half] for k in range(half)]
    total = received[0]
    for extra in received[1:]:
        total = total + extra
    total = lax.optimization_barrier(
        jnp.broadcast_to(jnp.sum(total, axis=1, keepdims=True), total.shape)
    )
    return total, got_down, got_up


def ionic_update(voltage, gating, conductance, gate_center, gate_slope, gate_rate, reversal):
    for substep in range(SUB):
        steady = jax.nn.sigmoid((voltage[None, :] - gate_center) / gate_slope)
        damping = jnp.exp(-gate_rate * (0.5 + steady))
        gating = steady + (gating - steady) * damping
        current = jnp.sum(conductance * gating * (voltage[None, :] - reversal), axis=0)
        voltage = voltage - current
    return (voltage, gating)


def body(
    states_old,
    coupling,
    gate_center,
    gate_slope,
    gate_rate,
    reversal,
    conductance,
    stimulus,
    coarse_rate,
):
    num_blocks = coupling.shape[0]
    tile_width = coupling.shape[2]
    zero_rows = jnp.zeros((2, tile_width), jnp.float32)

    def couple_local(vector, upper_rows):
        extended = jnp.concatenate([vector, upper_rows], axis=0)
        ahead_sum = jnp.sum(
            coupling[:, 0] * extended[1 : num_blocks + 1, None, :]
            + coupling[:, 1] * extended[2 : num_blocks + 2, None, :],
            axis=-1,
        )
        carried = jnp.sum(coupling * vector[:, None, :, None], axis=2)
        inner = jnp.concatenate([zero_rows[:1], carried[:-1, 0]], axis=0) + jnp.concatenate(
            [zero_rows, carried[:-2, 1]], axis=0
        )
        spilled = jnp.stack([carried[-1, 0] + carried[-2, 1], carried[-1, 1]])
        return ahead_sum + inner, spilled

    def pad_head(rows):
        return jnp.concatenate(
            [rows, jnp.zeros((num_blocks - 2, tile_width), jnp.float32)], axis=0
        )

    space_count = lax.axis_size("space")
    on_last = lax.axis_index("space") == space_count - 1
    on_first = lax.axis_index("space") == 0

    def couple_part(vector, upper_rows):
        partial, spilled = couple_local(vector, upper_rows)
        return partial, jnp.where(on_last, jnp.zeros_like(spilled), spilled)

    ones = jnp.ones((num_blocks, tile_width), jnp.float32)
    ones_up = jnp.where(on_last, jnp.zeros_like(ones[:2]), ones[:2])
    local_degree, spilled = couple_part(ones, ones_up)
    degree = local_degree + pad_head(passed_along(spilled, "space", 1))

    def solve(right_side, side_steps=()):
        side_steps = list(side_steps)
        side_state = side_steps.pop(0)(None) if side_steps else None
        upper = passed_along(right_side[:2], "space", -1)
        partial, spilled = couple_part(right_side, upper)
        local_mapped = right_side + degree * right_side - partial
        arrived = passed_along(spilled, "space", 1)
        mapped_up = passed_along(local_mapped[:2], "space", -1) - spilled
        residual = right_side - (local_mapped - pad_head(arrived))
        residual_up = upper - mapped_up
        iterate = right_side
        for iteration in range(CG_ITERS):
            partial, spilled = couple_part(residual, residual_up)
            local_image = residual + degree * residual - partial
            norm_part = jnp.sum(residual * residual, axis=0)
            energy_part = jnp.sum(residual * local_image, axis=0) - jnp.sum(
                residual_up * spilled, axis=0
            )
            sent_up = jnp.where(on_first, jnp.zeros_like(spilled), local_image[:2])
            sums, arrived, image_up = exchange(
                jnp.stack([norm_part, energy_part]), "space", spilled, sent_up
            )
            norm_now, energy = sums[0:1], sums[1:2]
            image = local_image - pad_head(arrived)
            image_up = image_up - spilled
            if iteration == 0:
                step_size = norm_now / energy
                direction, direction_up = residual, residual_up
                mapped, mapped_up = image, image_up
            else:
                ratio = norm_now / norm_before
                step_size = norm_now / (energy - ratio * norm_now / step_before)
                direction = residual + ratio * direction
                direction_up = residual_up + ratio * direction_up
                mapped = image + ratio * mapped
                mapped_up = image_up + ratio * mapped_up
            iterate = iterate + step_size * direction
            residual = residual - step_size * mapped
            residual_up = residual_up - step_size * mapped_up
            norm_before, step_before = norm_now, step_size
            if side_state is not None and iteration in (0, 1, 4, CG_ITERS - 1):
                side_state, residual, residual_up, iterate = lax.optimization_barrier(
                    (side_state, residual, residual_up, iterate)
                )
                if side_steps:
                    side_state = side_steps.pop(0)(side_state)
        for step in side_steps:
            side_state = step(side_state)
        return iterate, side_state

    slices = lax.axis_size("tm")
    assert slices & (slices - 1) == 0

    def scan_steps(rows, rates, exponent):
        def first(_):
            return shifted(jnp.concatenate([exponent[None, :], rows], axis=0), "tm", 1)

        def doubling(span):
            def step(packed):
                earlier = shifted(packed, "tm", span)
                decay = jnp.exp(-rates * packed[0][None, :])
                return jnp.concatenate(
                    [(packed[0] + earlier[0])[None, :], decay * earlier[1:] + packed[1:]],
                    axis=0,
                )

            return step

        steps = [first]
        span = 1
        while span < slices:
            steps.append(doubling(span))
            span *= 2
        return steps

    def cyclic_scan(rows, rates, exponent):
        packed = None
        for step in scan_steps(rows, rates, exponent):
            packed = step(packed)
        return packed[1:], packed[0]

    exponent = 1.0 + jax.nn.sigmoid(states_old[0, 0])
    factor = jnp.exp(-coarse_rate * exponent[None, :])

    voltage = states_old[0, 0]
    gating = states_old[0, 1:]
    for fine_step in range(FINE):
        voltage, gating = ionic_update(
            voltage, gating, conductance, gate_center, gate_slope, gate_rate, reversal
        )
        side_steps = ()
        if fine_step == FINE - 1:
            side_steps = scan_steps(
                gating - factor[1:] * states_old[0, 1:], coarse_rate[1:], exponent
            )
        voltage = voltage + stimulus[0]
        voltage, gating_scan = solve(voltage.reshape(num_blocks, tile_width), side_steps)
        voltage = voltage.reshape(-1)
    gating_rows = gating_scan[1:]
    voltage_offset = voltage - factor[0] * states_old[0, 0]
    voltage_row, total_exponent = cyclic_scan(voltage_offset[None, :], coarse_rate[:1], exponent)
    loop_a = jnp.exp(-coarse_rate * total_exponent[None, :])
    new_state = jnp.concatenate([voltage_row, gating_rows], axis=0) / (1.0 - loop_a)
    return (new_state[None], new_state[0][None])


def solution(mesh):
    return jax.shard_map(
        body,
        mesh=mesh,
        in_specs=(
            P("tm", None, "space"),
            P("space", None, None, None),
            P(),
            P(),
            P(),
            P(),
            P(None, "space"),
            P("tm", "space"),
            P(None, "space"),
        ),
        out_specs=(P("tm", None, "space"), P("tm", "space")),
        check_vma=False,
    )
```
